128 devices in a mesh: row: 16 (over y, z_lo, core), col: 8 (over z_hi, x).
Axes of the slice: x: 4, y: 4, z: 4 (z_hi: 2, z_lo: 2; z = z_hi * 2 + z_lo), core: 2. Of those that a mesh axis runs over, the one named last changes fastest.
Arguments:
- z_trunk: bfloat16 [1024, 1024, 128], P('row', 'col'), may hold values from -6 to 6
- coords: int32 [3, 1024], P(None, ('row', 'col')), may hold values from 0 to 255
- token_mask: int32 [1024], P(('row', 'col')), may hold values 0 or 1
- w_dist: bfloat16 [39, 128], replicated, may hold values from -6 to 6
- w_attn: bfloat16 [128, 512], replicated, may hold values from -0.5 to 0.5
- w_bias: bfloat16 [128, 4], replicated, may hold values from -100 to 100
- w_out: bfloat16 [128, 128], replicated, may hold values from -2 to 2
- w_pae: bfloat16 [128, 64], replicated, may hold values from -0.5 to 0.5
- w_pde: bfloat16 [128, 64], replicated, may hold values from -0.5 to 0.5
Outputs:
- logits: float32 [1024, 1024, 128], P('row', 'col')
The draws below stay inside these ranges and needn't reach their ends.
All inputs are finite; a program needn't handle non-finite values. No bound on the sum of `token_mask` on one device may be relied on, other than what follows from the above.
Results may differ from the reference program's by a relative error of at most 0.0055.
The reference program's roundings to bfloat16 on the way count: a program that leaves them out, or rounds other values in their place, can miss the bound.
Values may be sent and summed in bfloat16 or wider, within the bound.
A program may use at most 192 MiB of HBM per device.

```python
import jax
import jax.numpy as jnp
from jax import lax

C = 128
H = 4
BINS = 64
DBINS = 39
N = 1024


def draw_w_bias(key, part):
    base = jax.random.normal(jax.random.fold_in(key, 11), (C, H), jnp.float32)
    order = jax.random.permutation(jax.random.fold_in(key, 12), H).astype(jnp.float32)
    levels = 0.6 * 2.0 ** (0.5 * order)
    scaled = base * levels[None, :] * C ** (-0.5)
    return jnp.clip(scaled, -100.0, 100.0).astype(jnp.bfloat16)


def place_ends(drawn, own_key, low, largest):
    index_at = [jax.random.randint(jax.random.fold_in(own_key, axis), (), 0, length) for axis, length in enumerate(drawn.shape)]
    longest = drawn.shape.index(max(drawn.shape))
    beside = index_at[:longest] + [(index_at[longest] + 1) % drawn.shape[longest]] + index_at[longest + 1:]
    return drawn.at[tuple(index_at)].set(low).at[tuple(beside)].set(largest)


def level_of(stream_key, shape, split, smallest, high):
    gain, own = 1.0, jax.random.fold_in(stream_key, 6)
    for dim, parts in split:
        draws = jnp.exp(jax.random.uniform(jax.random.fold_in(own, dim), (parts,), jnp.float32, smallest / len(split), high / len(split)))
        gain = gain * jnp.repeat(draws, shape[dim] // parts).reshape([-1 if axis == dim else 1 for axis in range(len(shape))])
    return gain


def bell_draw(own_key, dims, spread, most, cuts=(), held_as=jnp.bfloat16):
    array = jax.random.normal(own_key, dims, jnp.float32) * spread
    if len(cuts) > 0:
        array = level_of(own_key, dims, cuts, -0.22, 0.18) * array
    return jnp.clip(array, min=-most, max=most).astype(held_as)


def setup_inputs(seed: int = 0) -> dict:
    splits = jax.random.split(jax.random.key(seed), 10)
    return {
        "z_trunk": bell_draw(splits[0], (N, N, C), 1.0, 6.0, ((0, 16), (1, 8))),
        "coords": place_ends(jax.random.randint(splits[1], (3, N), 0, 256), jax.random.fold_in(splits[1], 1), 0, 255).astype(jnp.int32),
        "token_mask": place_ends((jax.random.randint(splits[2], (N,), 0, 8) < 7).astype(jnp.int32), jax.random.fold_in(splits[2], 1), 0, 1),
        "w_dist": bell_draw(splits[3], (DBINS, C), 1.0, 6.0),
        "w_attn": bell_draw(splits[4], (C, 4 * C), C ** -0.5, 0.5),
        "w_bias": draw_w_bias(jax.random.fold_in(splits[9], 71), 0),
        "w_out": bell_draw(splits[6], (C, C), 0.35, 2.0),
        "w_pae": bell_draw(splits[7], (C, BINS), C ** -0.5, 0.5),
        "w_pde": bell_draw(splits[8], (C, BINS), C ** -0.5, 0.5),
    }


def layer_norm(values):
    widened = values.astype(jnp.float32)
    average = lax.optimization_barrier(jnp.mean(widened, axis=-1, keepdims=True))
    centred = widened - average
    variance = lax.optimization_barrier(jnp.mean(centred * centred, axis=-1, keepdims=True))
    return (centred * lax.rsqrt(variance + 1e-05)).astype(jnp.bfloat16)

def distance_bins(coord_rows, coord_cols, class_count):
    offsets = coord_rows[:, :, None] - coord_cols[:, None, :]
    squared = lax.optimization_barrier(jnp.sum(offsets * offsets, axis=0))
    bin_edges = 27 + 4 * jnp.arange(class_count - 1, dtype=jnp.int32)
    above = (squared[:, :, None] > (bin_edges * bin_edges)[None, None, :]).astype(jnp.int32)
    return lax.optimization_barrier(jnp.sum(above, axis=-1))

def attend_column(query_rows, key_rows, value_rows, bias_full, key_bias):
    length_all = query_rows.shape[0]
    block_rows = min(512, length_all)

    def one_block(first_row):
        query_block = lax.dynamic_slice_in_dim(query_rows, first_row, block_rows, 0).astype(jnp.float32)
        bias_block = lax.dynamic_slice_in_dim(bias_full, first_row, block_rows, 2)
        scores = jnp.einsum('khd,ihd->hki', key_rows.astype(jnp.float32), query_block)
        scores = scores + bias_block + key_bias[None, :, None]
        highest = lax.optimization_barrier(jnp.max(scores, axis=1, keepdims=True))
        raised = jnp.exp(scores - highest)
        weights = (raised / lax.optimization_barrier(jnp.sum(raised, axis=1, keepdims=True))).astype(jnp.bfloat16)
        return jnp.einsum('hki,khd->ihd', weights.astype(jnp.float32), value_rows.astype(jnp.float32))
    starts = jnp.arange(length_all // block_rows, dtype=jnp.int32) * block_rows
    blocks_out = lax.map(one_block, starts)
    return blocks_out.reshape(length_all, query_rows.shape[1], query_rows.shape[2])

def reference(z_trunk, coords, token_mask, w_dist, w_attn, w_bias, w_out, w_pae, w_pde):
    total = z_trunk.shape[0]
    width = z_trunk.shape[2]
    heads = w_bias.shape[1]
    head_dim = width // heads
    bins_all = distance_bins(coords, coords, w_dist.shape[0])
    pair = (z_trunk.astype(jnp.float32) + w_dist.astype(jnp.float32)[bins_all]).astype(jnp.bfloat16)
    normed = layer_norm(pair)
    bias_flat = jnp.dot(normed.reshape(-1, width), w_bias, preferred_element_type=jnp.float32)
    bias_full = bias_flat.reshape(total, total, heads).transpose(2, 0, 1)
    key_bias = (token_mask.astype(jnp.float32) - 1.0) * 30000.0

    def one_column(operands):
        normed_col, pair_col = operands
        projected = jnp.dot(normed_col, w_attn, preferred_element_type=jnp.float32)
        query_rows = (projected[:, :width] * head_dim ** (-0.5)).astype(jnp.bfloat16).reshape(total, heads, head_dim)
        key_rows = projected[:, width:2 * width].astype(jnp.bfloat16).reshape(total, heads, head_dim)
        value_rows = projected[:, 2 * width:3 * width].astype(jnp.bfloat16).reshape(total, heads, head_dim)
        gate_rows = projected[:, 3 * width:].astype(jnp.bfloat16)
        attended = attend_column(query_rows, key_rows, value_rows, bias_full, key_bias).reshape(total, width)
        gated = (jax.nn.sigmoid(gate_rows.astype(jnp.float32)) * attended).astype(jnp.bfloat16)
        update = jnp.dot(gated, w_out, preferred_element_type=jnp.float32)
        return (pair_col.astype(jnp.float32) + update).astype(jnp.bfloat16)
    updated_swapped = lax.map(one_column, (jnp.swapaxes(normed, 0, 1), jnp.swapaxes(pair, 0, 1)))
    updated = jnp.swapaxes(updated_swapped, 0, 1)
    symmetric = updated.astype(jnp.float32) + jnp.swapaxes(updated, 0, 1).astype(jnp.float32)
    pae_part = jnp.dot(layer_norm(updated).reshape(-1, width), w_pae, preferred_element_type=jnp.float32)
    pde_part = jnp.dot(layer_norm(symmetric).reshape(-1, width), w_pde, preferred_element_type=jnp.float32)
    return jnp.concatenate([pae_part, pde_part], axis=1).reshape(total, total, -1)
```

```python
import functools

import jax
import jax.numpy as jnp
from jax import lax
from jax.experimental import pallas as pl
from jax.experimental.pallas import tpu as pltpu
from jax.sharding import PartitionSpec as P

MESH = pl.DeviceIdType.MESH
BF = jnp.bfloat16
F32 = jnp.float32
LOG2E = 1.4426950408889634
ORDERS = (("y", "z", "x"), ("z", "x", "y"), ("x", "y", "z"))
ROWS = ((0, 24), (24, 24), (48, 16))


def layer_norm(values):
    widened = values.astype(F32)
    average = jnp.mean(widened, axis=-1, keepdims=True)
    centred = widened - average
    variance = jnp.mean(centred * centred, axis=-1, keepdims=True)
    return (centred * lax.rsqrt(variance + 1e-05)).astype(BF)


def remote(src, dst, send, recv, device):
    return pltpu.make_async_remote_copy(
        src_ref=src, dst_ref=dst, send_sem=send, recv_sem=recv, device_id=device, device_id_type=MESH
    )


def embed_kernel(z_ref, sub_ref, lane_ref, wd_ref, wb_ref, pair_ref, bias_ref,
                 rs, rl, flat, s_send, s_recv, l_send, l_recv):
    row = lax.axis_index("row")
    col = lax.axis_index("col")
    slot = lax.rem(row, 2) * 8 + col
    target = row // 2
    barrier = pltpu.get_barrier_semaphore()

    def greet_row(d, _):
        pl.semaphore_signal(barrier, inc=1, device_id=(row, lax.rem(col + d, 8)), device_id_type=MESH)
        return 0

    lax.fori_loop(1, 8, greet_row, 0)

    def greet_source(s, _):
        src_row = 2 * col + s // 8
        src_col = lax.rem(s, 8)

        @pl.when(jnp.logical_or(src_row != row, src_col != col))
        def _():
            pl.semaphore_signal(barrier, inc=1, device_id=(src_row, src_col), device_id_type=MESH)

        return 0

    lax.fori_loop(0, 16, greet_source, 0)

    @pl.when(target == col)
    def _():
        pl.semaphore_wait(barrier, 22)

    @pl.when(target != col)
    def _():
        pl.semaphore_wait(barrier, 23)

    def row_copy(d):
        to = lax.rem(col + d, 8)
        return remote(sub_ref, rs.at[col], s_send.at[d - 1], s_recv.at[d - 1], (row, to))

    def lane_copy(r):
        return remote(lane_ref, rl.at[slot], l_send.at[r], l_recv.at[slot], (r, target))

    def lane_arrival(s):
        return remote(lane_ref, rl.at[s], l_send.at[s], l_recv.at[s], (2 * col + s // 8, lax.rem(s, 8)))

    def start_row(d, _):
        row_copy(d).start()
        return 0

    lax.fori_loop(1, 8, start_row, 0)

    def start_lane(r, _):
        @pl.when(jnp.logical_or(r != row, target != col))
        def _():
            lane_copy(r).start()

        return 0

    lax.fori_loop(0, 16, start_lane, 0)
    rs[col] = sub_ref[...]

    @pl.when(target == col)
    def _():
        rl[slot] = lane_ref[...]

    def wait_row(d, _):
        row_copy(d).wait()
        return 0

    lax.fori_loop(1, 8, wait_row, 0)

    def wait_lane(r, _):
        @pl.when(jnp.logical_or(r != row, target != col))
        def _():
            lane_copy(r).wait_send()

        @pl.when(jnp.logical_or(2 * col + r // 8 != row, lax.rem(r, 8) != col))
        def _():
            lane_arrival(r).wait_recv()

        return 0

    lax.fori_loop(0, 16, wait_lane, 0)

    lanes = jnp.sum(rl[...], axis=0)
    cx, cy, cz = lanes[0:1], lanes[1:2], lanes[2:3]
    edge = lax.broadcasted_iota(jnp.int32, (40, 128), 0)
    upper_edge = 27 + 4 * edge
    lower_edge = 23 + 4 * edge
    big = jnp.int32(1 << 20)
    lower = jnp.where(edge == 0, -1, jnp.where(edge == 39, big, lower_edge * lower_edge)).astype(F32)
    upper = jnp.where(edge >= 38, big, upper_edge * upper_edge).astype(F32)
    wd = wd_ref[...]
    wb = wb_ref[...]

    def eight(t, _):
        own = rs[t]
        dx = own[:, 0:1] - cx
        dy = own[:, 1:2] - cy
        dz = own[:, 2:3] - cz
        squared = dx * dx + dy * dy + dz * dz
        key_bias = (own[:, 3:4] - 1.0) * 30000.0
        rows = []
        for a in range(8):
            i = t * 8 + a
            here = jnp.broadcast_to(squared[a : a + 1], (40, 128))
            hot = jnp.where(jnp.logical_and(here > lower, here <= upper), 1.0, 0.0).astype(BF)
            added = lax.dot_general(hot, wd, (((0,), (0,)), ((), ())), preferred_element_type=F32)
            pair = (z_ref[i].astype(F32) + added).astype(BF)
            flat[pl.ds(i, 128, stride=64), :] = pair.astype(F32)
            normed = layer_norm(pair)
            b = lax.dot_general(wb, normed, (((1,), (1,)), ((), ())), preferred_element_type=F32)
            rows.append(b + key_bias[a : a + 1])
        start = pl.multiple_of(t * 8, 8)
        for h in range(4):
            bias_ref[h, pl.ds(start, 8), :] = jnp.concatenate([r[h : h + 1] for r in rows], axis=0)
        return 0

    lax.fori_loop(0, 8, eight, 0)

    def out(g, _):
        for j in range(8):
            at = pl.multiple_of((g * 8 + j) * 64, 64)
            pair_ref[g, j] = flat[pl.ds(at, 64), :].astype(BF)
        return 0

    lax.fori_loop(0, 16, out, 0)


def embed(z, sub, lane, wd, wb):
    return pl.pallas_call(
        embed_kernel,
        out_shape=(
            jax.ShapeDtypeStruct((16, 8, 64, 128), BF),
            jax.ShapeDtypeStruct((4, 64, 128), F32),
        ),
        in_specs=[pl.BlockSpec(memory_space=pltpu.VMEM)] * 5,
        out_specs=(pl.BlockSpec(memory_space=pltpu.VMEM),) * 2,
        scratch_shapes=[
            pltpu.VMEM((8, 8, 128), F32),
            pltpu.VMEM((16, 8, 128), F32),
            pltpu.VMEM((8192, 128), F32),
            pltpu.SemaphoreType.DMA((7,)),
            pltpu.SemaphoreType.DMA((7,)),
            pltpu.SemaphoreType.DMA((16,)),
            pltpu.SemaphoreType.DMA((16,)),
        ],
        compiler_params=pltpu.CompilerParams(collective_id=0, has_side_effects=True, vmem_limit_bytes=40 << 20),
        name="embed",
    )(z, sub, lane, wd, wb)


def place():
    row = lax.axis_index("row")
    col = lax.axis_index("col")
    core = lax.rem(row, 2)
    at = {"x": lax.rem(col, 4), "y": row // 4, "z": (col // 4) * 2 + lax.rem(row // 2, 2)}
    return row, col, core, at


def device_of(at, core):
    return (at["y"] * 4 + lax.rem(at["z"], 2) * 2 + core, (at["z"] // 2) * 4 + at["x"])


def beside(at, dim, delta):
    moved = dict(at)
    moved[dim] = lax.rem(at[dim] + delta + 4, 4)
    return moved


def entry_kernel(pair_ref, bias_ref, out_ref, g0, g1, g2, own_v, send, recv, psend, precv, lsem, asend, arecv, osem):
    row, col, core, at = place()
    gs = (g0, g1, g2)
    partner = device_of(at, 1 - core)
    barrier = pltpu.get_barrier_semaphore()

    def greet(d, _):
        pl.semaphore_signal(barrier, inc=1, device_id=(lax.rem(row + d, 16), col), device_id_type=MESH)
        return 0

    lax.fori_loop(1, 16, greet, 0)
    for dim in ("x", "y", "z"):
        for delta in (1, -1):
            pl.semaphore_signal(barrier, inc=1, device_id=device_of(beside(at, dim, delta), core), device_id_type=MESH)
    pl.semaphore_wait(barrier, 21)

    def a2a(d):
        to = lax.rem(row + d, 16)
        return remote(pair_ref.at[to], out_ref.at[row], asend.at[d - 1], arecv.at[d - 1], (to, col))

    load_own = pltpu.make_async_copy(pair_ref.at[row], own_v, osem.at[0])
    load_own.start()
    pending = []
    partner_waits = []

    def to_partner(p, n, src, dst):
        c = remote(src, dst, psend.at[p, n], precv.at[p, n], partner)
        c.start()
        partner_waits.append(c)

    locals_ = []
    firsts = {}

    def begin(stage, p):
        dims = ORDERS[p]
        a1, a2, a3 = (at[d] for d in dims)
        first, count = ROWS[p]
        g = gs[p]
        if stage == 0:
            src = bias_ref.at[:, pl.ds(first, count), :]
            dst = g.at[core, a3, a2, a1]
            keep = pltpu.make_async_copy(src, dst, lsem.at[p])
            keep.start()
            locals_.append(keep)
            to_partner(p, 0, src, dst)
        elif stage == 1:
            src = dst = g.at[core, a3, a2]
        else:
            src = dst = g.at[core, a3]
        d = dims[stage]
        for k, delta in enumerate((1, -1)):
            c = remote(src, dst, send.at[p, stage * 4 + k], recv.at[p, stage * 4 + k],
                       device_of(beside(at, d, delta), core))
            c.start()
            pending.append(c)
            firsts[stage, p, k] = c

    def block(stage, p, delta):
        dims = ORDERS[p]
        a = [at[d] for d in dims]
        a[stage] = lax.rem(a[stage] + delta + 4, 4)
        a1, a2, a3 = a
        g = gs[p]
        if stage == 0:
            return g.at[core, a3, a2, a1]
        if stage == 1:
            return g.at[core, a3, a2]
        return g.at[core, a3]

    def forward(stage, p):
        d = ORDERS[p][stage]
        for k, delta in enumerate((1, -1)):
            firsts[stage, p, k].wait_recv()
            got = block(stage, p, -delta)
            half = got.at[pl.ds(2 * k, 2)]
            c = remote(half, half, send.at[p, stage * 4 + 2 + k], recv.at[p, stage * 4 + 2 + k],
                       device_of(beside(at, d, delta), core))
            c.start()
            pending.append(c)
            firsts[stage, p, 2 + k] = c
            to_partner(p, 1 + stage * 4 + k, got, got)

    def finish(stage, p):
        for k in (0, 1):
            firsts[stage, p, 2 + k].wait_recv()
            half = block(stage, p, 2).at[pl.ds(2 * k, 2)]
            to_partner(p, 3 + stage * 4 + k, half, half)

    def start_a2a(first, last):
        def go(d, _):
            a2a(d).start()
            return 0

        lax.fori_loop(first, last, go, 0)

    for p in range(3):
        begin(0, p)
    for p in range(3):
        forward(0, p)
    for p in range(3):
        finish(0, p)
    for c in locals_:
        c.wait()
    for p in range(3):
        begin(1, p)
    start_a2a(1, 16)
    load_own.wait()
    save_own = pltpu.make_async_copy(own_v, out_ref.at[row], osem.at[1])
    save_own.start()
    for p in range(3):
        forward(1, p)
    for p in range(3):
        finish(1, p)
    for p in range(3):
        begin(2, p)
    for p in range(3):
        forward(2, p)
    for p in range(3):
        finish(2, p)
    save_own.wait()

    def wait_a2a(d, _):
        a2a(d).wait()
        return 0

    lax.fori_loop(1, 16, wait_a2a, 0)
    for c in partner_waits:
        c.wait()
    for c in pending:
        c.wait_send()


def entry(pair, bias):
    any_spec = pl.BlockSpec(memory_space=pl.ANY)
    return pl.pallas_call(
        entry_kernel,
        out_shape=(jax.ShapeDtypeStruct((16, 8, 64, 128), BF),)
        + tuple(jax.ShapeDtypeStruct((2, 4, 4, 4, 4, n, 128), F32) for _, n in ROWS),
        in_specs=[any_spec, pl.BlockSpec(memory_space=pltpu.VMEM)],
        out_specs=(any_spec,) * 4,
        scratch_shapes=[
            pltpu.VMEM((8, 64, 128), BF),
            pltpu.SemaphoreType.DMA((3, 12)),
            pltpu.SemaphoreType.DMA((3, 12)),
            pltpu.SemaphoreType.DMA((3, 13)),
            pltpu.SemaphoreType.DMA((3, 13)),
            pltpu.SemaphoreType.DMA((3,)),
            pltpu.SemaphoreType.DMA((15,)),
            pltpu.SemaphoreType.DMA((15,)),
            pltpu.SemaphoreType.DMA((2,)),
        ],
        compiler_params=pltpu.CompilerParams(collective_id=1, has_side_effects=True),
        name="entry",
    )(pair, bias)


def attn_kernel(x_ref, b0, b1, b2, wa_ref, wo_ref, o_ref, q_s, k_s, v_s, g_s, s_s, a_s):
    step = pl.program_id(0)

    @pl.when(step == 0)
    def _():
        def one(j, _):
            p = jnp.dot(layer_norm(x_ref[:, j].reshape(1024, 128)), wa_ref[...], preferred_element_type=F32)
            q_s[j] = (p[:, :128] * (32**-0.5)).astype(BF)
            k_s[j] = p[:, 128:256].astype(BF)
            v_s[j] = p[:, 256:384].astype(BF).T
            g_s[j] = p[:, 384:].astype(BF)
            return 0

        lax.fori_loop(0, 8, one, 0)

    head_of_lane = lax.broadcasted_iota(jnp.int32, (256, 128), 1) // 32
    ones = jnp.ones((16, 256), BF)
    i0 = pl.multiple_of(step * 256, 256)
    bs = (b0, b1, b2)

    def bias_piece(kb, h, x):
        parts = []
        for zl in range(2):
            for core in range(2):
                for p in range(3):
                    where = {"x": x, "y": kb, "z": zl}
                    d1, d2, d3 = ORDERS[p]
                    parts.append(bs[p][core, where[d3], where[d2], where[d1], h])
        return jnp.concatenate(parts, axis=0)

    def one(j, _):
        q = q_s[j, pl.ds(i0, 256), :]
        for h in range(4):
            qm = jnp.where(head_of_lane == h, q, jnp.zeros_like(q))
            mx = None
            for kb in range(4):
                s = lax.dot_general(k_s[j, pl.ds(kb * 256, 256), :], qm, (((1,), (1,)), ((), ())),
                                    preferred_element_type=F32)
                s = s + jnp.concatenate([bias_piece(kb, h, 0), bias_piece(kb, h, 1)], axis=1)
                s_s[h % 2, kb] = s
                t = jnp.max(s.reshape(32, 8, 256), axis=0)
                mx = t if mx is None else jnp.maximum(mx, t)
            m = jnp.max(mx, axis=0, keepdims=True)
            acc = None
            for kb in range(4):
                d = (s_s[h % 2, kb] - m) * LOG2E
                p = jnp.exp2(d.astype(BF))
                lhs = jnp.concatenate([v_s[j, h * 32 : h * 32 + 32, kb * 256 : kb * 256 + 256], ones], axis=0)
                r = jnp.dot(lhs, p, preferred_element_type=F32)
                acc = r if acc is None else acc + r
            a_s[h * 32 : h * 32 + 32] = acc[:32] / acc[32:33]
        att = a_s[...].T
        g = g_s[j, pl.ds(i0, 256), :].astype(F32)
        gated = (att / (1.0 + jnp.exp(-g))).astype(BF)
        upd = jnp.dot(gated, wo_ref[...], preferred_element_type=F32)
        x = x_ref[pl.ds(step * 4, 4), j].reshape(256, 128)
        o_ref[j] = (x.astype(F32) + upd).astype(BF)
        return 0

    lax.fori_loop(0, 8, one, 0)


def attend(x, gs, wa, wo):
    def bias_spec(p):
        d1, d2, d3 = ORDERS[p]
        size = {"x": 2, "y": 4, "z": 2}

        def index(c):
            pick = {"x": c % 2, "y": 0, "z": c // 2}
            return (0, pick[d3], pick[d2], pick[d1], 0, 0, 0)

        return pl.BlockSpec((2, size[d3], size[d2], size[d1], 4, ROWS[p][1], 128), index)

    return pl.pallas_call(
        attn_kernel,
        grid=(4,),
        out_shape=jax.ShapeDtypeStruct((8, 1024, 128), BF),
        in_specs=[
            pl.BlockSpec((16, 8, 64, 128), lambda c: (0, 0, 0, 0)),
            bias_spec(0),
            bias_spec(1),
            bias_spec(2),
            pl.BlockSpec((128, 512), lambda c: (0, 0)),
            pl.BlockSpec((128, 128), lambda c: (0, 0)),
        ],
        out_specs=pl.BlockSpec((8, 256, 128), lambda c: (0, c, 0)),
        scratch_shapes=[
            pltpu.VMEM((8, 1024, 128), BF),
            pltpu.VMEM((8, 1024, 128), BF),
            pltpu.VMEM((8, 128, 1024), BF),
            pltpu.VMEM((8, 1024, 128), BF),
            pltpu.VMEM((2, 4, 256, 256), F32),
            pltpu.VMEM((128, 256), F32),
        ],
        compiler_params=pltpu.CompilerParams(vmem_limit_bytes=60 << 20),
        name="attend",
    )(x, *gs, wa, wo)


def exit_kernel(u_ref, d_ref, m_ref, own_d, own_m, dsend, drecv, msend, mrecv, osem):
    row = lax.axis_index("row")
    col = lax.axis_index("col")
    to_row = 2 * col + row // 8
    slot = lax.rem(row, 8)
    src_col = row // 2
    src_row0 = lax.rem(row, 2) * 8
    barrier = pltpu.get_barrier_semaphore()

    def greet(d, _):
        pl.semaphore_signal(barrier, inc=1, device_id=(lax.rem(row + d, 16), col), device_id_type=MESH)
        return 0

    lax.fori_loop(1, 16, greet, 0)
    mine = jnp.logical_and(to_row == row, True)

    def greet_source(s, _):
        @pl.when(jnp.logical_or(src_row0 + s != row, src_col != col))
        def _():
            pl.semaphore_signal(barrier, inc=1, device_id=(src_row0 + s, src_col), device_id_type=MESH)

        return 0

    lax.fori_loop(0, 8, greet_source, 0)

    @pl.when(mine)
    def _():
        pl.semaphore_wait(barrier, 22)

    @pl.when(jnp.logical_not(mine))
    def _():
        pl.semaphore_wait(barrier, 23)

    def direct(d):
        to = lax.rem(row + d, 16)
        return remote(u_ref.at[:, pl.ds(pl.multiple_of(to * 64, 64), 64), :], d_ref.at[row],
                      dsend.at[d - 1], drecv.at[d - 1], (to, col))

    def mirror(c):
        return remote(u_ref.at[:, pl.ds(pl.multiple_of(c * 128, 128), 128), :], m_ref.at[slot],
                      msend.at[c], mrecv.at[slot], (to_row, c))

    def arrival(s):
        return remote(u_ref.at[:, pl.ds(0, 128), :], m_ref.at[s], msend.at[s], mrecv.at[s], (src_row0 + s, src_col))

    def start_mirror(t, _):
        c = lax.rem(col + t, 8)

        @pl.when(jnp.logical_or(to_row != row, c != col))
        def _():
            mirror(c).start()

        return 0

    def start_direct(d, _):
        direct(d).start()
        return 0

    lax.fori_loop(0, 8, start_mirror, 0)
    lax.fori_loop(1, 16, start_direct, 0)
    in_d = pltpu.make_async_copy(u_ref.at[:, pl.ds(pl.multiple_of(row * 64, 64), 64), :], own_d, osem.at[0])
    in_d.start()
    in_d.wait()
    out_d = pltpu.make_async_copy(own_d, d_ref.at[row], osem.at[1])
    out_d.start()

    @pl.when(mine)
    def _():
        in_m = pltpu.make_async_copy(u_ref.at[:, pl.ds(pl.multiple_of(col * 128, 128), 128), :], own_m, osem.at[2])
        in_m.start()
        in_m.wait()
        out_m = pltpu.make_async_copy(own_m, m_ref.at[slot], osem.at[3])
        out_m.start()
        out_m.wait()

    out_d.wait()

    def wait_direct(d, _):
        direct(d).wait()
        return 0

    lax.fori_loop(1, 16, wait_direct, 0)

    def wait_mirror(s, _):
        @pl.when(jnp.logical_or(to_row != row, s != col))
        def _():
            mirror(s).wait_send()

        @pl.when(jnp.logical_or(src_row0 + s != row, src_col != col))
        def _():
            arrival(s).wait_recv()

        return 0

    lax.fori_loop(0, 8, wait_mirror, 0)


def leave(u):
    any_spec = pl.BlockSpec(memory_space=pl.ANY)
    return pl.pallas_call(
        exit_kernel,
        out_shape=(jax.ShapeDtypeStruct((16, 8, 64, 128), BF), jax.ShapeDtypeStruct((8, 8, 128, 128), BF)),
        in_specs=[any_spec],
        out_specs=(any_spec,) * 2,
        scratch_shapes=[
            pltpu.VMEM((8, 64, 128), BF),
            pltpu.VMEM((8, 128, 128), BF),
            pltpu.SemaphoreType.DMA((15,)),
            pltpu.SemaphoreType.DMA((15,)),
            pltpu.SemaphoreType.DMA((8,)),
            pltpu.SemaphoreType.DMA((8,)),
            pltpu.SemaphoreType.DMA((4,)),
        ],
        compiler_params=pltpu.CompilerParams(collective_id=2, has_side_effects=True),
        name="leave",
    )(u)


def logits_kernel(d_ref, m_ref, wp_ref, we_ref, o_ref, flat):
    step = pl.program_id(0)

    @pl.when(step == 0)
    def _():
        def widen(g, _):
            for j in range(8):
                at = pl.multiple_of((g * 8 + j) * 64, 64)
                flat[pl.ds(at, 64), :] = d_ref[g, j].astype(F32)
            return 0

        lax.fori_loop(0, 16, widen, 0)

    for a in range(8):
        u = flat[pl.ds(step * 8 + a, 128, stride=64), :]
        sym = u + m_ref[a].astype(F32)
        pae = jnp.dot(layer_norm(u), wp_ref[...], preferred_element_type=F32)
        pde = jnp.dot(layer_norm(sym), we_ref[...], preferred_element_type=F32)
        o_ref[a] = pae + pde


def logits(d, m, wp, we):
    return pl.pallas_call(
        logits_kernel,
        grid=(8,),
        out_shape=jax.ShapeDtypeStruct((64, 128, 128), F32),
        in_specs=[
            pl.BlockSpec((16, 8, 64, 128), lambda t: (0, 0, 0, 0)),
            pl.BlockSpec((8, 128, 128), lambda t: (t, 0, 0)),
            pl.BlockSpec((128, 128), lambda t: (0, 0)),
            pl.BlockSpec((128, 128), lambda t: (0, 0)),
        ],
        out_specs=pl.BlockSpec((8, 128, 128), lambda t: (t, 0, 0)),
        scratch_shapes=[pltpu.VMEM((8192, 128), F32)],
        compiler_params=pltpu.CompilerParams(vmem_limit_bytes=40 << 20),
        name="logits",
    )(d, m, wp, we)


def per_device(z_trunk, coords, token_mask, w_dist, w_attn, w_bias, w_out, w_pae, w_pde):
    device = lax.axis_index("row") * 8 + lax.axis_index("col")
    info = jnp.concatenate([coords, token_mask[None]], axis=0).astype(F32)
    sub = jnp.pad(info.T, ((0, 0), (0, 124)))
    lane = jnp.arange(128, dtype=jnp.int32)[None, :] // 8 == lax.rem(device, 16)
    lane = jnp.where(lane, jnp.tile(info, (2, 16)), 0.0)
    wd = jnp.pad(w_dist, ((0, 1), (0, 0)))
    wb = jnp.pad(w_bias.T, ((0, 4), (0, 0)))
    pair, bias = embed(z_trunk, sub, lane, wd, wb)
    columns, *gs = entry(pair, bias)
    updated = attend(columns, gs, w_attn, w_out)
    direct, mirror = leave(updated)
    wp = jnp.pad(w_pae, ((0, 0), (0, 64)))
    we = jnp.pad(w_pde, ((0, 0), (64, 0)))
    return logits(direct, mirror.reshape(64, 128, 128), wp, we)


def solution(mesh):
    in_specs = (P("row", "col", None), P(None, ("row", "col")), P(("row", "col")), P(), P(), P(), P(), P(), P())
    return jax.shard_map(
        per_device, mesh=mesh, in_specs=in_specs, out_specs=P("row", "col", None), check_vma=False
    )
```

```python
import functools

import jax
import jax.numpy as jnp
from jax import lax
from jax.experimental import pallas as pl
from jax.experimental.pallas import tpu as pltpu
from jax.sharding import PartitionSpec as P

MESH = pl.DeviceIdType.MESH
BF = jnp.bfloat16
F32 = jnp.float32
LOG2E = 1.4426950408889634
ORDERS = (("y", "z", "x"), ("z", "x", "y"), ("x", "y", "z"))
ROWS = ((0, 24), (24, 24), (48, 16))


def layer_norm(values):
    widened = values.astype(F32)
    average = jnp.mean(widened, axis=-1, keepdims=True)
    centred = widened - average
    variance = jnp.mean(centred * centred, axis=-1, keepdims=True)
    return (centred * lax.rsqrt(variance + 1e-05)).astype(BF)


def remote(src, dst, send, recv, device):
    return pltpu.make_async_remote_copy(
        src_ref=src, dst_ref=dst, send_sem=send, recv_sem=recv, device_id=device, device_id_type=MESH
    )


def embed_kernel(z_ref, sub_ref, lane_ref, wd_ref, wb_ref, pair_ref, bias_ref,
                 rs, rl, flat, s_send, s_recv, l_send, l_recv):
    row = lax.axis_index("row")
    col = lax.axis_index("col")
    slot = lax.rem(row, 2) * 8 + col
    target = row // 2
    barrier = pltpu.get_barrier_semaphore()

    def greet_row(d, _):
        pl.semaphore_signal(barrier, inc=1, device_id=(row, lax.rem(col + d, 8)), device_id_type=MESH)
        return 0

    lax.fori_loop(1, 8, greet_row, 0)

    def greet_source(s, _):
        src_row = 2 * col + s // 8
        src_col = lax.rem(s, 8)

        @pl.when(jnp.logical_or(src_row != row, src_col != col))
        def _():
            pl.semaphore_signal(barrier, inc=1, device_id=(src_row, src_col), device_id_type=MESH)

        return 0

    lax.fori_loop(0, 16, greet_source, 0)

    @pl.when(target == col)
    def _():
        pl.semaphore_wait(barrier, 22)

    @pl.when(target != col)
    def _():
        pl.semaphore_wait(barrier, 23)

    def row_copy(d):
        to = lax.rem(col + d, 8)
        return remote(sub_ref, rs.at[col], s_send.at[d - 1], s_recv.at[d - 1], (row, to))

    def lane_copy(r):
        return remote(lane_ref, rl.at[slot], l_send.at[r], l_recv.at[slot], (r, target))

    def lane_arrival(s):
        return remote(lane_ref, rl.at[s], l_send.at[s], l_recv.at[s], (2 * col + s // 8, lax.rem(s, 8)))

    def start_row(d, _):
        row_copy(d).start()
        return 0

    lax.fori_loop(1, 8, start_row, 0)

    def start_lane(r, _):
        @pl.when(jnp.logical_or(r != row, target != col))
        def _():
            lane_copy(r).start()

        return 0

    lax.fori_loop(0, 16, start_lane, 0)
    rs[col] = sub_ref[...]

    @pl.when(target == col)
    def _():
        rl[slot] = lane_ref[...]

    def wait_row(d, _):
        row_copy(d).wait()
        return 0

    lax.fori_loop(1, 8, wait_row, 0)

    def wait_lane(r, _):
        @pl.when(jnp.logical_or(r != row, target != col))
        def _():
            lane_copy(r).wait_send()

        @pl.when(jnp.logical_or(2 * col + r // 8 != row, lax.rem(r, 8) != col))
        def _():
            lane_arrival(r).wait_recv()

        return 0

    lax.fori_loop(0, 16, wait_lane, 0)

    lanes = jnp.sum(rl[...], axis=0)
    cx, cy, cz = lanes[0:1], lanes[1:2], lanes[2:3]
    edge = lax.broadcasted_iota(jnp.int32, (40, 128), 0)
    upper_edge = 27 + 4 * edge
    lower_edge = 23 + 4 * edge
    big = jnp.int32(1 << 20)
    lower = jnp.where(edge == 0, -1, jnp.where(edge == 39, big, lower_edge * lower_edge)).astype(F32)
    upper = jnp.where(edge >= 38, big, upper_edge * upper_edge).astype(F32)
    wd = wd_ref[...]
    wb = wb_ref[...]

    head = lax.broadcasted_iota(jnp.int32, (8, 128), 1) // 32

    def eight(t, _):
        own = rs[t]
        dx = own[:, 0:1] - cx
        dy = own[:, 1:2] - cy
        dz = own[:, 2:3] - cz
        squared = dx * dx + dy * dy + dz * dz
        key_bias = (own[:, 3:4] - 1.0) * 30000.0
        rows = []
        for a in range(8):
            i = t * 8 + a
            here = jnp.broadcast_to(squared[a : a + 1], (40, 128))
            hot = jnp.where(jnp.logical_and(here > lower, here <= upper), 1.0, 0.0).astype(BF)
            added = lax.dot_general(hot, wd, (((0,), (0,)), ((), ())), preferred_element_type=F32)
            pair = (z_ref[i].astype(F32) + added).astype(BF)
            flat[pl.ds(i, 128, stride=64), :] = pair.astype(F32)
            normed = layer_norm(pair)
            b = lax.dot_general(wb, normed, (((1,), (1,)), ((), ())), preferred_element_type=F32)
            rows.append(b + key_bias[a : a + 1])
        start = pl.multiple_of(t * 8, 8)
        by_head = [jnp.concatenate([r[h : h + 1] for r in rows], axis=0) for h in range(4)]
        for c in range(4):
            moved = [pltpu.roll(by_head[h], (32 * h - 32 * c) % 128, 1) for h in range(4)]
            block = moved[3]
            for h in (2, 1, 0):
                block = jnp.where(head == h, moved[h], block)
            bias_ref[c, pl.ds(start, 8), :] = block
        return 0

    lax.fori_loop(0, 8, eight, 0)

    def out(g, _):
        for j in range(8):
            at = pl.multiple_of((g * 8 + j) * 64, 64)
            pair_ref[g, j] = flat[pl.ds(at, 64), :].astype(BF)
        return 0

    lax.fori_loop(0, 16, out, 0)


def embed(z, sub, lane, wd, wb):
    return pl.pallas_call(
        embed_kernel,
        out_shape=(
            jax.ShapeDtypeStruct((16, 8, 64, 128), BF),
            jax.ShapeDtypeStruct((4, 64, 128), F32),
        ),
        in_specs=[pl.BlockSpec(memory_space=pltpu.VMEM)] * 5,
        out_specs=(pl.BlockSpec(memory_space=pltpu.VMEM),) * 2,
        scratch_shapes=[
            pltpu.VMEM((8, 8, 128), F32),
            pltpu.VMEM((16, 8, 128), F32),
            pltpu.VMEM((8192, 128), F32),
            pltpu.SemaphoreType.DMA((7,)),
            pltpu.SemaphoreType.DMA((7,)),
            pltpu.SemaphoreType.DMA((16,)),
            pltpu.SemaphoreType.DMA((16,)),
        ],
        compiler_params=pltpu.CompilerParams(collective_id=0, has_side_effects=True, vmem_limit_bytes=40 << 20),
        name="embed",
    )(z, sub, lane, wd, wb)


def place():
    row = lax.axis_index("row")
    col = lax.axis_index("col")
    core = lax.rem(row, 2)
    at = {"x": lax.rem(col, 4), "y": row // 4, "z": (col // 4) * 2 + lax.rem(row // 2, 2)}
    return row, col, core, at


def device_of(at, core):
    return (at["y"] * 4 + lax.rem(at["z"], 2) * 2 + core, (at["z"] // 2) * 4 + at["x"])


def beside(at, dim, delta):
    moved = dict(at)
    moved[dim] = lax.rem(at[dim] + delta + 4, 4)
    return moved


def of32(n):
    return pl.multiple_of(n, 32)


def main_kernel(pair_ref, bias_ref, wa_ref, wo_ref, d_ref, m_ref,
                xs, g0, g1, g2, q_s, k_s, v_s, g_s, s_s, u_s, relay,
                asend, arecv, osem, send, recv, lsem, psend, precv,
                dsend, drecv, rsend, rrecv, msend, mrecv, hsem):
    row, col, core, at = place()
    gs = (g0, g1, g2)
    zh = col // 4
    yh = row // 8
    partner = device_of(at, 1 - core)
    opposite = device_of(beside(at, "x", 2), core)
    looped = jnp.logical_and(yh == zh, core == yh)
    src_row0 = core * 8
    src_zh = yh
    slot = lax.rem(row, 8)
    barrier = pltpu.get_barrier_semaphore()

    def signal(device):
        pl.semaphore_signal(barrier, inc=1, device_id=device, device_id_type=MESH)

    def greet(d, _):
        signal((lax.rem(row + d, 16), col))
        return 0

    lax.fori_loop(1, 16, greet, 0)
    for dim in ("x", "y", "z"):
        for delta in (1, -1):
            signal(device_of(beside(at, dim, delta), core))
    signal(opposite)

    def greet_relay(s, _):
        @pl.when(jnp.logical_or(src_row0 + s != row, src_zh != zh))
        def _():
            signal((src_row0 + s, src_zh * 4 + at["x"]))

        return 0

    lax.fori_loop(0, 8, greet_relay, 0)

    @pl.when(looped)
    def _():
        pl.semaphore_wait(barrier, 29)

    @pl.when(jnp.logical_not(looped))
    def _():
        pl.semaphore_wait(barrier, 30)

    def a2a(d):
        to = lax.rem(row + d, 16)
        return remote(pair_ref.at[to], xs.at[row], asend.at[d - 1], arecv.at[d - 1], (to, col))

    def start_a2a(first, last):
        def go(d, _):
            a2a(d).start()
            return 0

        lax.fori_loop(first, last, go, 0)

    def gather_copy(stage, p, k, t):
        dims = ORDERS[p]
        first, count = ROWS[p]
        g = gs[p]
        delta = (1, -1)[k % 2]
        a = [at[d] for d in dims]
        if k >= 2:
            a[stage] = lax.rem(a[stage] - delta + 4, 4)
        a1, a2, a3 = a
        half = pl.ds(2 * (k % 2), 2)
        if stage == 0:
            dst = g.at[t, core, a3, a2, a1]
            src = bias_ref.at[t, pl.ds(first, count), :] if k < 2 else dst
            if k >= 2:
                part = pl.ds(0, 8) if k == 2 else pl.ds(8, count - 8)
                src = dst = dst.at[part]
        else:
            src = g.at[t, core, a3, a2] if stage == 1 else g.at[t, core, a3]
            if k >= 2:
                src = src.at[half]
            dst = src
        n = p * 12 + stage * 4 + k
        return remote(src, dst, send.at[t, n], recv.at[t, n], device_of(beside(at, dims[stage], delta), core))

    def keep(p, t):
        a1, a2, a3 = (at[d] for d in ORDERS[p])
        first, count = ROWS[p]
        return pltpu.make_async_copy(
            bias_ref.at[t, pl.ds(first, count), :], gs[p].at[t, core, a3, a2, a1], lsem.at[t, p]
        )

    def share(p, t):
        half = gs[p].at[t, core]
        return remote(half, half, psend.at[t, p], precv.at[t, p], partner)

    def gather_step(n, t):
        parts = range(3)
        if n == 0:
            for p in parts:
                keep(p, t).start()
                for k in (0, 1):
                    gather_copy(0, p, k, t).start()
        elif n in (1, 3, 5):
            stage = n // 2
            for p in parts:
                for k in (0, 1):
                    gather_copy(stage, p, k, t).wait_recv()
                    gather_copy(stage, p, k + 2, t).start()
        elif n in (2, 4):
            stage = n // 2
            for p in parts:
                if n == 2:
                    keep(p, t).wait()
                for k in (2, 3):
                    gather_copy(stage - 1, p, k, t).wait_recv()
                for k in (0, 1):
                    gather_copy(stage, p, k, t).start()
        elif n == 6:
            for p in parts:
                for k in (2, 3):
                    gather_copy(2, p, k, t).wait_recv()
                share(p, t).start()
        else:
            for p in parts:
                share(p, t).wait()
                for stage in range(3):
                    for k in range(4):
                        gather_copy(stage, p, k, t).wait_send()

    def direct(c, t):
        to = 2 * c + t // 2
        return (
            to,
            u_s.at[:, pl.ds(of32(c * 128 + t * 32), 32), :],
            d_ref.at[row, :, pl.ds(of32(lax.rem(t, 2) * 32), 32), :],
            dsend.at[t, c],
            drecv.at[lax.rem(t, 2), row],
        )

    def direct_remote(c, t):
        to, src, dst, s1, s2 = direct(c, t)
        return remote(src, dst, s1, s2, (to, col))

    def direct_local(c, t):
        to, src, dst, s1, s2 = direct(c, t)
        return pltpu.make_async_copy(src, dst, hsem.at[0, lax.rem(t, 2)])

    def direct_arrival(s, tt):
        return remote(
            u_s.at[:, pl.ds(0, 32), :], d_ref.at[s, :, pl.ds(of32(tt * 32), 32), :],
            dsend.at[0, 0], drecv.at[tt, s], (s, col),
        )

    def hop(delta, zz, t):
        x2 = lax.rem(at["x"] + delta, 4)
        c = zz * 4 + x2
        return remote(
            u_s.at[:, pl.ds(of32(c * 128 + t * 32), 32), :], relay.at[t, 3 - delta, zz],
            rsend.at[t, delta - 1, zz], rrecv.at[t, 3 - delta, zz], device_of(beside(at, "x", delta), core),
        )

    def hop_arrival(n, zz, t):
        return remote(
            u_s.at[:, pl.ds(0, 32), :], relay.at[t, n, zz],
            rsend.at[t, 2 - n, zz], rrecv.at[t, n, zz], device_of(beside(at, "x", n + 1), core),
        )

    def mirror(n, zz, t):
        sx = lax.rem(at["x"] + n, 4)
        to_row = 2 * (4 * zh + sx) + yh
        c = zz * 4 + at["x"]
        if n == 0:
            src = u_s.at[:, pl.ds(of32(c * 128 + t * 32), 32), :]
        else:
            src = relay.at[t, n - 1, zz]
        dst = m_ref.at[slot, :, pl.ds(of32(t * 32), 32), :]
        here = jnp.logical_and(to_row == row, zz == zh)
        rem = remote(src, dst, msend.at[t, n, zz], mrecv.at[t, slot], (to_row, c))
        loc = pltpu.make_async_copy(src, dst, hsem.at[1, t])
        return here, rem, loc

    def mirror_arrival(s, t):
        return remote(
            u_s.at[:, pl.ds(0, 32), :], m_ref.at[s, :, pl.ds(of32(t * 32), 32), :],
            msend.at[t, 0, 0], mrecv.at[t, s], (src_row0 + s, src_zh * 4 + at["x"]),
        )

    def either(here, if_here, otherwise):
        @pl.when(here)
        def _():
            if_here()

        @pl.when(jnp.logical_not(here))
        def _():
            otherwise()

    def exit_first(t):
        for zz in range(2):
            for delta in (1, 2, 3):
                hop(delta, zz, t).start()
        for zz in range(2):
            here, rem, loc = mirror(0, zz, t)
            either(here, loc.start, rem.start)

        def go(n, _):
            c = lax.rem(col + n, 8)
            either(
                2 * c + t // 2 == row, lambda: direct_local(c, t).start(), lambda: direct_remote(c, t).start()
            )
            return 0

        lax.fori_loop(0, 8, go, 0)

    def exit_second(t):
        for n in (1, 2, 3):
            for zz in range(2):
                hop_arrival(n - 1, zz, t).wait_recv()
                here, rem, loc = mirror(n, zz, t)
                either(here, loc.start, rem.start)

    def project(j):
        p = jnp.dot(layer_norm(xs[:, j].reshape(1024, 128)), wa_ref[...], preferred_element_type=F32)
        q_s[j] = (p[:, :128] * (32**-0.5)).astype(BF)
        k_s[j] = p[:, 128:256].astype(BF)
        v_s[j] = p[:, 256:384].astype(BF).T
        g_s[j] = p[:, 384:].astype(BF)

    head_of_lane = lax.broadcasted_iota(jnp.int32, (32, 128), 1) // 32
    ones = jnp.ones((16, 256), BF)

    def bias_block(t, cp, kb, n):
        parts = []
        for zl in range(2):
            for cc in range(2):
                for p in range(3):
                    where = {"x": 2 * lax.rem(cp, 2) + n, "y": kb, "z": 2 * (cp // 2) + zl}
                    d1, d2, d3 = ORDERS[p]
                    parts.append(gs[p][t, cc, where[d3], where[d2], where[d1]])
        return jnp.concatenate(parts, axis=0)

    def task(t, cp, j):
        parts = []
        for n in range(2):
            q = q_s[j, pl.ds(of32((cp * 2 + n) * 128 + t * 32), 32), :]
            for h in range(4):
                parts.append(jnp.where(head_of_lane == h, q, jnp.zeros_like(q)))
        qm = jnp.concatenate(parts, axis=0)
        mx = None
        for kb in range(4):
            s = lax.dot_general(k_s[j, pl.ds(kb * 256, 256), :], qm, (((1,), (1,)), ((), ())),
                                preferred_element_type=F32)
            s = s + jnp.concatenate([bias_block(t, cp, kb, 0), bias_block(t, cp, kb, 1)], axis=1)
            s_s[kb] = s
            m = jnp.max(s.reshape(32, 8, 256), axis=0)
            mx = m if mx is None else jnp.maximum(mx, m)
        m = jnp.max(mx, axis=0, keepdims=True)
        acc = None
        for kb in range(4):
            e = jnp.exp2(((s_s[kb] - m) * LOG2E).astype(BF))
            lhs = jnp.concatenate([v_s[j, :, kb * 256 : kb * 256 + 256], ones], axis=0)
            r = jnp.dot(lhs, e, preferred_element_type=F32)
            acc = r if acc is None else acc + r
        att = acc[:128] * (1.0 / acc[128:129])
        for n in range(2):
            a = att[:, n * 128 : n * 128 + 128].T
            rows = a[96:128]
            for h in (2, 1, 0):
                rows = jnp.where(head_of_lane == h, a[h * 32 : h * 32 + 32], rows)
            first = of32((cp * 2 + n) * 128 + t * 32)
            gate = g_s[j, pl.ds(first, 32), :].astype(F32)
            gated = (rows / (1.0 + jnp.exp(-gate))).astype(BF)
            upd = jnp.dot(gated, wo_ref[...], preferred_element_type=F32)
            x = xs[(cp * 2 + n) * 2 + t // 2, j, pl.ds(of32(lax.rem(t, 2) * 32), 32), :]
            u_s[j, pl.ds(first, 32), :] = (x.astype(F32) + upd).astype(BF)

    own = pltpu.make_async_copy(pair_ref.at[row], xs.at[row], osem)
    own.start()
    gather_step(0, 0)
    for n in range(1, 6):
        start_a2a(3 * n - 2, 3 * n + 1)
        gather_step(n, 0)
    own.wait()

    def wait_a2a(d, _):
        a2a(d).wait()
        return 0

    lax.fori_loop(1, 16, wait_a2a, 0)
    gather_step(6, 0)

    def prepare(j, _):
        for n in range(8):
            @pl.when(j == n)
            def _():
                gather_step(n, 1)

        project(j)
        return 0

    lax.fori_loop(0, 8, prepare, 0)
    gather_step(7, 0)

    def chunk(t, _):
        def half(hh, _):
            for n in range(8):
                @pl.when(jnp.logical_and(hh == n, t < 2))
                def _():
                    gather_step(n, t + 2)

            @pl.when(jnp.logical_and(hh == 0, t > 0))
            def _():
                exit_first(t - 1)

            @pl.when(jnp.logical_and(hh == 3, t > 0))
            def _():
                exit_second(t - 1)

            def column(j, _):
                task(t, hh // 2, lax.rem(hh, 2) * 4 + j)
                return 0

            lax.fori_loop(0, 4, column, 0)
            return 0

        lax.fori_loop(0, 8, half, 0)
        return 0

    lax.fori_loop(0, 4, chunk, 0)
    exit_first(3)
    exit_second(3)

    def drain(t, _):
        def one(c, _):
            either(
                2 * c + t // 2 == row, lambda: direct_local(c, t).wait(), lambda: direct_remote(c, t).wait_send()
            )
            return 0

        lax.fori_loop(0, 8, one, 0)
        for zz in range(2):
            for delta in (1, 2, 3):
                hop(delta, zz, t).wait_send()
            for n in range(4):
                here, rem, loc = mirror(n, zz, t)
                either(here, loc.wait, rem.wait_send)

        def arrived(s, _):
            @pl.when(jnp.logical_or(src_row0 + s != row, src_zh != zh))
            def _():
                mirror_arrival(s, t).wait_recv()

            return 0

        lax.fori_loop(0, 8, arrived, 0)
        return 0

    lax.fori_loop(0, 4, drain, 0)

    def landed(s, _):
        @pl.when(s != row)
        def _():
            for tt in range(2):
                direct_arrival(s, tt).wait_recv()

        return 0

    lax.fori_loop(0, 16, landed, 0)


def main(pair, bias, wa, wo):
    any_spec = pl.BlockSpec(memory_space=pl.ANY)
    vmem = pl.BlockSpec(memory_space=pltpu.VMEM)
    dma = pltpu.SemaphoreType.DMA
    return pl.pallas_call(
        main_kernel,
        out_shape=(jax.ShapeDtypeStruct((16, 8, 64, 128), BF), jax.ShapeDtypeStruct((8, 8, 128, 128), BF)),
        in_specs=[any_spec, vmem, vmem, vmem],
        out_specs=(any_spec,) * 2,
        scratch_shapes=[pltpu.VMEM((16, 8, 64, 128), BF)]
        + [pltpu.VMEM((4, 2, 4, 4, 4, n, 128), F32) for _, n in ROWS]
        + [
            pltpu.VMEM((8, 1024, 128), BF),
            pltpu.VMEM((8, 1024, 128), BF),
            pltpu.VMEM((8, 128, 1024), BF),
            pltpu.VMEM((8, 1024, 128), BF),
            pltpu.VMEM((4, 256, 256), F32),
            pltpu.VMEM((8, 1024, 128), BF),
            pltpu.VMEM((4, 3, 2, 8, 32, 128), BF),
            dma((15,)), dma((15,)), dma,
            dma((4, 36)), dma((4, 36)), dma((4, 3)), dma((4, 3)), dma((4, 3)),
            dma((4, 8)), dma((2, 16)), dma((4, 3, 2)), dma((4, 3, 2)), dma((4, 4, 2)), dma((4, 8)), dma((2, 4)),
        ],
        compiler_params=pltpu.CompilerParams(collective_id=1, has_side_effects=True, vmem_limit_bytes=60 << 20),
        name="main",
    )(pair, bias, wa, wo)


def logits_kernel(d_ref, m_ref, wp_ref, we_ref, o_ref, flat):
    step = pl.program_id(0)

    @pl.when(step == 0)
    def _():
        def widen(g, _):
            for j in range(8):
                at = pl.multiple_of((g * 8 + j) * 64, 64)
                flat[pl.ds(at, 64), :] = d_ref[g, j].astype(F32)
            return 0

        lax.fori_loop(0, 16, widen, 0)

    for a in range(8):
        u = flat[pl.ds(step * 8 + a, 128, stride=64), :]
        sym = u + m_ref[a].astype(F32)
        pae = jnp.dot(layer_norm(u), wp_ref[...], preferred_element_type=F32)
        pde = jnp.dot(layer_norm(sym), we_ref[...], preferred_element_type=F32)
        o_ref[a] = pae + pde


def logits(d, m, wp, we):
    return pl.pallas_call(
        logits_kernel,
        grid=(8,),
        out_shape=jax.ShapeDtypeStruct((64, 128, 128), F32),
        in_specs=[
            pl.BlockSpec((16, 8, 64, 128), lambda t: (0, 0, 0, 0)),
            pl.BlockSpec((8, 128, 128), lambda t: (t, 0, 0)),
            pl.BlockSpec((128, 128), lambda t: (0, 0)),
            pl.BlockSpec((128, 128), lambda t: (0, 0)),
        ],
        out_specs=pl.BlockSpec((8, 128, 128), lambda t: (t, 0, 0)),
        scratch_shapes=[pltpu.VMEM((8192, 128), F32)],
        compiler_params=pltpu.CompilerParams(vmem_limit_bytes=40 << 20),
        name="logits",
    )(d, m, wp, we)


def per_device(z_trunk, coords, token_mask, w_dist, w_attn, w_bias, w_out, w_pae, w_pde):
    device = lax.axis_index("row") * 8 + lax.axis_index("col")
    info = jnp.concatenate([coords, token_mask[None]], axis=0).astype(F32)
    sub = jnp.pad(info.T, ((0, 0), (0, 124)))
    lane = jnp.arange(128, dtype=jnp.int32)[None, :] // 8 == lax.rem(device, 16)
    lane = jnp.where(lane, jnp.tile(info, (2, 16)), 0.0)
    wd = jnp.pad(w_dist, ((0, 1), (0, 0)))
    wb = jnp.pad(w_bias.T, ((0, 4), (0, 0)))
    pair, bias = embed(z_trunk, sub, lane, wd, wb)
    direct, mirror = main(pair, bias, w_attn, w_out)
    wp = jnp.pad(w_pae, ((0, 0), (0, 64)))
    we = jnp.pad(w_pde, ((0, 0), (64, 0)))
    return logits(direct, mirror.reshape(64, 128, 128), wp, we)


def solution(mesh):
    in_specs = (P("row", "col", None), P(None, ("row", "col")), P(("row", "col")), P(), P(), P(), P(), P(), P())
    return jax.shard_map(
        per_device, mesh=mesh, in_specs=in_specs, out_specs=P("row", "col", None), check_vma=False
    )
```

```python
import functools

import jax
import jax.numpy as jnp
from jax import lax
from jax.experimental import pallas as pl
from jax.experimental.pallas import tpu as pltpu
from jax.sharding import PartitionSpec as P

MESH = pl.DeviceIdType.MESH
BF = jnp.bfloat16
F32 = jnp.float32
LOG2E = 1.4426950408889634
ORDERS = (("y", "z", "x"), ("z", "x", "y"), ("x", "y", "z"))
ROWS = ((0, 24), (24, 24), (48, 16))
SPREAD = (
    (1, 0, 0), (3, 0, 0), (0, 1, 0), (2, 0, 0), (1, 1, 0), (3, 1, 0), (0, 0, 1), (2, 1, 0),
    (1, 0, 1), (3, 0, 1), (0, 1, 1), (2, 0, 1), (1, 1, 1), (3, 1, 1), (2, 1, 1),
)
PREPARE = {0: (1, 3), 2: (2, 0), 4: (1, 4), 6: (2, 1)}
ATTEND = {
    (0, 0): (1, 5), (0, 1): (2, 2), (0, 2): (1, 6), (0, 3): (2, 3), (0, 4): (1, 7), (0, 5): (2, 4), (0, 6): (3, 0),
    (0, 7): (2, 5), (1, 0): (3, 1), (1, 1): (2, 6), (1, 2): (3, 2), (1, 3): (2, 7), (1, 4): (3, 3), (1, 6): (3, 4),
    (2, 0): (3, 5), (2, 2): (3, 6), (2, 4): (3, 7),
}


def layer_norm(values):
    widened = values.astype(F32)
    average = jnp.mean(widened, axis=-1, keepdims=True)
    centred = widened - average
    variance = jnp.mean(centred * centred, axis=-1, keepdims=True)
    return (centred * lax.rsqrt(variance + 1e-05)).astype(BF)


def remote(src, dst, send, recv, device):
    return pltpu.make_async_remote_copy(
        src_ref=src, dst_ref=dst, send_sem=send, recv_sem=recv, device_id=device, device_id_type=MESH
    )


def embed_kernel(z_ref, sub_ref, lane_ref, wd_ref, wb_ref, pair_ref, bias_ref,
                 rs, rl, flat, s_send, s_recv, l_send, l_recv):
    row = lax.axis_index("row")
    col = lax.axis_index("col")
    slot = lax.rem(row, 2) * 8 + col
    target = row // 2
    barrier = pltpu.get_barrier_semaphore()

    def greet_row(d, _):
        pl.semaphore_signal(barrier, inc=1, device_id=(row, lax.rem(col + d, 8)), device_id_type=MESH)
        return 0

    lax.fori_loop(1, 8, greet_row, 0)

    def greet_source(s, _):
        src_row = 2 * col + s // 8
        src_col = lax.rem(s, 8)

        @pl.when(jnp.logical_or(src_row != row, src_col != col))
        def _():
            pl.semaphore_signal(barrier, inc=1, device_id=(src_row, src_col), device_id_type=MESH)

        return 0

    lax.fori_loop(0, 16, greet_source, 0)

    @pl.when(target == col)
    def _():
        pl.semaphore_wait(barrier, 22)

    @pl.when(target != col)
    def _():
        pl.semaphore_wait(barrier, 23)

    def row_copy(d):
        to = lax.rem(col + d, 8)
        return remote(sub_ref, rs.at[col], s_send.at[d - 1], s_recv.at[d - 1], (row, to))

    def lane_copy(r):
        return remote(lane_ref, rl.at[slot], l_send.at[r], l_recv.at[slot], (r, target))

    def lane_arrival(s):
        return remote(lane_ref, rl.at[s], l_send.at[s], l_recv.at[s], (2 * col + s // 8, lax.rem(s, 8)))

    def start_row(d, _):
        row_copy(d).start()
        return 0

    lax.fori_loop(1, 8, start_row, 0)

    def start_lane(r, _):
        @pl.when(jnp.logical_or(r != row, target != col))
        def _():
            lane_copy(r).start()

        return 0

    lax.fori_loop(0, 16, start_lane, 0)
    rs[col] = sub_ref[...]

    @pl.when(target == col)
    def _():
        rl[slot] = lane_ref[...]

    def wait_row(d, _):
        row_copy(d).wait()
        return 0

    lax.fori_loop(1, 8, wait_row, 0)

    def wait_lane(r, _):
        @pl.when(jnp.logical_or(r != row, target != col))
        def _():
            lane_copy(r).wait_send()

        @pl.when(jnp.logical_or(2 * col + r // 8 != row, lax.rem(r, 8) != col))
        def _():
            lane_arrival(r).wait_recv()

        return 0

    lax.fori_loop(0, 16, wait_lane, 0)

    lanes = jnp.sum(rl[...], axis=0)
    cx, cy, cz = lanes[0:1], lanes[1:2], lanes[2:3]
    edge = lax.broadcasted_iota(jnp.int32, (40, 128), 0)
    upper_edge = 27 + 4 * edge
    lower_edge = 23 + 4 * edge
    big = jnp.int32(1 << 20)
    lower = jnp.where(edge == 0, -1, jnp.where(edge == 39, big, lower_edge * lower_edge)).astype(F32)
    upper = jnp.where(edge >= 38, big, upper_edge * upper_edge).astype(F32)
    wd = wd_ref[...]
    wb = wb_ref[...]

    head = lax.broadcasted_iota(jnp.int32, (8, 128), 1) // 32

    def eight(t, _):
        own = rs[t]
        dx = own[:, 0:1] - cx
        dy = own[:, 1:2] - cy
        dz = own[:, 2:3] - cz
        squared = dx * dx + dy * dy + dz * dz
        key_bias = (own[:, 3:4] - 1.0) * 30000.0
        rows = []
        for a in range(8):
            i = t * 8 + a
            here = jnp.broadcast_to(squared[a : a + 1], (40, 128))
            hot = jnp.where(jnp.logical_and(here > lower, here <= upper), 1.0, 0.0).astype(BF)
            added = lax.dot_general(hot, wd, (((0,), (0,)), ((), ())), preferred_element_type=F32)
            pair = (z_ref[i].astype(F32) + added).astype(BF)
            flat[pl.ds(i, 128, stride=64), :] = pair.astype(F32)
            normed = layer_norm(pair)
            b = lax.dot_general(wb, normed, (((1,), (1,)), ((), ())), preferred_element_type=F32)
            rows.append(b + key_bias[a : a + 1])
        start = pl.multiple_of(t * 8, 8)
        by_head = [jnp.concatenate([r[h : h + 1] for r in rows], axis=0) for h in range(4)]
        for c in range(4):
            moved = [pltpu.roll(by_head[h], (32 * h - 32 * c) % 128, 1) for h in range(4)]
            block = moved[3]
            for h in (2, 1, 0):
                block = jnp.where(head == h, moved[h], block)
            bias_ref[c, pl.ds(start, 8), :] = block
        return 0

    lax.fori_loop(0, 8, eight, 0)

    def out(g, _):
        for j in range(8):
            at = pl.multiple_of((g * 8 + j) * 64, 64)
            pair_ref[g, j] = flat[pl.ds(at, 64), :].astype(BF)
        return 0

    lax.fori_loop(0, 16, out, 0)


def embed(z, sub, lane, wd, wb):
    return pl.pallas_call(
        embed_kernel,
        out_shape=(
            jax.ShapeDtypeStruct((16, 8, 64, 128), BF),
            jax.ShapeDtypeStruct((4, 64, 128), F32),
        ),
        in_specs=[pl.BlockSpec(memory_space=pltpu.VMEM)] * 5,
        out_specs=(pl.BlockSpec(memory_space=pltpu.VMEM),) * 2,
        scratch_shapes=[
            pltpu.VMEM((8, 8, 128), F32),
            pltpu.VMEM((16, 8, 128), F32),
            pltpu.VMEM((8192, 128), F32),
            pltpu.SemaphoreType.DMA((7,)),
            pltpu.SemaphoreType.DMA((7,)),
            pltpu.SemaphoreType.DMA((16,)),
            pltpu.SemaphoreType.DMA((16,)),
        ],
        compiler_params=pltpu.CompilerParams(collective_id=0, has_side_effects=True, vmem_limit_bytes=40 << 20),
        name="embed",
    )(z, sub, lane, wd, wb)


def place():
    row = lax.axis_index("row")
    col = lax.axis_index("col")
    core = lax.rem(row, 2)
    at = {"x": lax.rem(col, 4), "y": row // 4, "z": (col // 4) * 2 + lax.rem(row // 2, 2)}
    return row, col, core, at


def device_of(at, core):
    return (at["y"] * 4 + lax.rem(at["z"], 2) * 2 + core, (at["z"] // 2) * 4 + at["x"])


def beside(at, dim, delta):
    moved = dict(at)
    moved[dim] = lax.rem(at[dim] + delta + 4, 4)
    return moved


def of32(n):
    return pl.multiple_of(n, 32)


def main_kernel(pair_ref, bias_ref, wa_ref, wo_ref, d_ref, m_ref,
                xs, g0, g1, g2, q_s, k_s, v_s, g_s, s_s, m_s, acc_s, u_s, relay,
                asend, arecv, osem, send, recv, lsem, psend, precv,
                dsend, drecv, rsend, rrecv, msend, mrecv, hsem):
    row, col, core, at = place()
    gs = (g0, g1, g2)
    zh = col // 4
    yh = row // 8
    partner = device_of(at, 1 - core)
    opposite = device_of(beside(at, "x", 2), core)
    looped = jnp.logical_and(yh == zh, core == yh)
    src_row0 = core * 8
    src_zh = yh
    slot = lax.rem(row, 8)
    barrier = pltpu.get_barrier_semaphore()

    def signal(device):
        pl.semaphore_signal(barrier, inc=1, device_id=device, device_id_type=MESH)

    def greet(d, _):
        signal((lax.rem(row + d, 16), col))
        return 0

    lax.fori_loop(1, 16, greet, 0)
    for dim in ("x", "y", "z"):
        for delta in (1, -1):
            signal(device_of(beside(at, dim, delta), core))
    signal(opposite)

    def greet_relay(s, _):
        @pl.when(jnp.logical_or(src_row0 + s != row, src_zh != zh))
        def _():
            signal((src_row0 + s, src_zh * 4 + at["x"]))

        return 0

    lax.fori_loop(0, 8, greet_relay, 0)

    @pl.when(looped)
    def _():
        pl.semaphore_wait(barrier, 29)

    @pl.when(jnp.logical_not(looped))
    def _():
        pl.semaphore_wait(barrier, 30)

    def a2a(n):
        dy, dz, dc = SPREAD[n]
        to = lax.rem(at["y"] + dy, 4) * 4 + lax.rem(lax.rem(row // 2, 2) + dz, 2) * 2 + lax.rem(core + dc, 2)
        return remote(pair_ref.at[to], xs.at[row], asend.at[n], arecv.at[n], (to, col))

    def gather_copy(stage, p, k, t):
        dims = ORDERS[p]
        first, count = ROWS[p]
        g = gs[p]
        delta = (1, -1)[k % 2]
        a = [at[d] for d in dims]
        if k >= 2:
            a[stage] = lax.rem(a[stage] - delta + 4, 4)
        a1, a2, a3 = a
        half = pl.ds(2 * (k % 2), 2)
        if stage == 0:
            dst = g.at[t, core, a3, a2, a1]
            src = bias_ref.at[t, pl.ds(first, count), :] if k < 2 else dst
            if k >= 2:
                part = pl.ds(0, 8) if k == 2 else pl.ds(8, count - 8)
                src = dst = dst.at[part]
        else:
            src = g.at[t, core, a3, a2] if stage == 1 else g.at[t, core, a3]
            if k >= 2:
                src = src.at[half]
            dst = src
        n = p * 12 + stage * 4 + k
        return remote(src, dst, send.at[t, n], recv.at[t, n], device_of(beside(at, dims[stage], delta), core))

    def keep(p, t):
        a1, a2, a3 = (at[d] for d in ORDERS[p])
        first, count = ROWS[p]
        return pltpu.make_async_copy(
            bias_ref.at[t, pl.ds(first, count), :], gs[p].at[t, core, a3, a2, a1], lsem.at[t, p]
        )

    def share(p, t):
        half = gs[p].at[t, core]
        return remote(half, half, psend.at[t, p], precv.at[t, p], partner)

    def gather_step(n, t):
        parts = range(3)
        if n == 0:
            for p in parts:
                keep(p, t).start()
                for k in (0, 1):
                    gather_copy(0, p, k, t).start()
        elif n in (1, 3, 5):
            stage = n // 2
            for p in parts:
                for k in (0, 1):
                    gather_copy(stage, p, k, t).wait_recv()
                    gather_copy(stage, p, k + 2, t).start()
        elif n in (2, 4):
            stage = n // 2
            for p in parts:
                if n == 2:
                    keep(p, t).wait()
                for k in (2, 3):
                    gather_copy(stage - 1, p, k, t).wait_recv()
                for k in (0, 1):
                    gather_copy(stage, p, k, t).start()
        elif n == 6:
            for p in parts:
                for k in (2, 3):
                    gather_copy(2, p, k, t).wait_recv()
                share(p, t).start()
        else:
            for p in parts:
                share(p, t).wait()
                for stage in range(3):
                    for k in range(4):
                        gather_copy(stage, p, k, t).wait_send()

    def direct(c, t):
        to = 2 * c + t // 2
        return (
            to,
            u_s.at[:, pl.ds(of32(c * 128 + t * 32), 32), :],
            d_ref.at[row, :, pl.ds(of32(lax.rem(t, 2) * 32), 32), :],
            dsend.at[t, c],
            drecv.at[lax.rem(t, 2), row],
        )

    def direct_remote(c, t):
        to, src, dst, s1, s2 = direct(c, t)
        return remote(src, dst, s1, s2, (to, col))

    def direct_local(c, t):
        to, src, dst, s1, s2 = direct(c, t)
        return pltpu.make_async_copy(src, dst, hsem.at[0, lax.rem(t, 2)])

    def direct_arrival(s, tt):
        return remote(
            u_s.at[:, pl.ds(0, 32), :], d_ref.at[s, :, pl.ds(of32(tt * 32), 32), :],
            dsend.at[0, 0], drecv.at[tt, s], (s, col),
        )

    def hop(delta, zz, t):
        x2 = lax.rem(at["x"] + delta, 4)
        c = zz * 4 + x2
        return remote(
            u_s.at[:, pl.ds(of32(c * 128 + t * 32), 32), :], relay.at[t, 3 - delta, zz],
            rsend.at[t, delta - 1, zz], rrecv.at[t, 3 - delta, zz], device_of(beside(at, "x", delta), core),
        )

    def hop_arrival(n, zz, t):
        return remote(
            u_s.at[:, pl.ds(0, 32), :], relay.at[t, n, zz],
            rsend.at[t, 2 - n, zz], rrecv.at[t, n, zz], device_of(beside(at, "x", n + 1), core),
        )

    def mirror(n, zz, t):
        sx = lax.rem(at["x"] + n, 4)
        to_row = 2 * (4 * zh + sx) + yh
        c = zz * 4 + at["x"]
        if n == 0:
            src = u_s.at[:, pl.ds(of32(c * 128 + t * 32), 32), :]
        else:
            src = relay.at[t, n - 1, zz]
        dst = m_ref.at[slot, :, pl.ds(of32(t * 32), 32), :]
        here = jnp.logical_and(to_row == row, zz == zh)
        rem = remote(src, dst, msend.at[t, n, zz], mrecv.at[t, slot], (to_row, c))
        loc = pltpu.make_async_copy(src, dst, hsem.at[1, t])
        return here, rem, loc

    def mirror_arrival(s, t):
        return remote(
            u_s.at[:, pl.ds(0, 32), :], m_ref.at[s, :, pl.ds(of32(t * 32), 32), :],
            msend.at[t, 0, 0], mrecv.at[t, s], (src_row0 + s, src_zh * 4 + at["x"]),
        )

    def either(here, if_here, otherwise):
        @pl.when(here)
        def _():
            if_here()

        @pl.when(jnp.logical_not(here))
        def _():
            otherwise()

    def exit_first(t):
        for zz in range(2):
            for delta in (1, 2, 3):
                hop(delta, zz, t).start()
        for zz in range(2):
            here, rem, loc = mirror(0, zz, t)
            either(here, loc.start, rem.start)

        def go(n, _):
            c = lax.rem(col + n, 8)
            either(
                2 * c + t // 2 == row, lambda: direct_local(c, t).start(), lambda: direct_remote(c, t).start()
            )
            return 0

        lax.fori_loop(0, 8, go, 0)

    def exit_second(t):
        for n in (1, 2, 3):
            for zz in range(2):
                hop_arrival(n - 1, zz, t).wait_recv()
                here, rem, loc = mirror(n, zz, t)
                either(here, loc.start, rem.start)

    def project(j):
        p = jnp.dot(layer_norm(xs[:, j].reshape(1024, 128)), wa_ref[...], preferred_element_type=F32)
        q_s[j] = (p[:, :128] * (32**-0.5)).astype(BF)
        k_s[j] = p[:, 128:256].astype(BF)
        v_s[j] = p[:, 256:384].astype(BF).T
        g_s[j] = p[:, 384:].astype(BF)

    head_of_lane = lax.broadcasted_iota(jnp.int32, (32, 128), 1) // 32
    ones = jnp.ones((16, 256), BF)

    def bias_block(t, cp, kb, n):
        parts = []
        for zl in range(2):
            for cc in range(2):
                for p in range(3):
                    where = {"x": 2 * lax.rem(cp, 2) + n, "y": kb, "z": 2 * (cp // 2) + zl}
                    d1, d2, d3 = ORDERS[p]
                    parts.append(gs[p][t, cc, where[d3], where[d2], where[d1]])
        return jnp.concatenate(parts, axis=0)

    diagonal = lax.broadcasted_iota(jnp.int32, (128, 256), 0) // 32 == lax.rem(
        lax.broadcasted_iota(jnp.int32, (128, 256), 1) // 32, 4
    )
    fold_row = lax.broadcasted_iota(jnp.int32, (64, 256), 0)
    fold_lane = lax.broadcasted_iota(jnp.int32, (64, 256), 1)
    fold = jnp.where(
        jnp.logical_and(fold_row // 32 == fold_lane // 128, lax.rem(fold_row, 32) == lax.rem(fold_lane, 32)), 1.0, 0.0
    ).astype(BF)
    minor = (((1,), (1,)), ((), ()))

    def split(f):
        return f // 32, lax.rem(f, 32) // 8, lax.rem(f, 8)

    def queries(t, cp, j):
        parts = []
        for n in range(2):
            q = q_s[j, pl.ds(of32((cp * 2 + n) * 128 + t * 32), 32), :]
            for h in range(4):
                parts.append(jnp.where(head_of_lane == h, q, jnp.zeros_like(q)))
        return jnp.concatenate(parts, axis=0)

    def score(t, cp, j, qm, kb):
        s = lax.dot_general(k_s[j, pl.ds(kb * 256, 256), :], qm, minor, preferred_element_type=F32)
        return s + jnp.concatenate([bias_block(t, cp, kb, 0), bias_block(t, cp, kb, 1)], axis=1)

    def score_block(b, t, cp, j, qm, kb, highest):
        s = score(t, cp, j, qm, kb)
        s_s[b, kb] = s
        here = jnp.max(s.reshape(32, 8, 256), axis=0)
        return here if highest is None else jnp.maximum(highest, here)

    def finish(t, cp, j, acc):
        att = jnp.where(diagonal, acc[:128] * (1.0 / acc[128:129]), 0.0)
        high = att.astype(BF)
        low = (att - high.astype(F32)).astype(BF)
        rows = lax.dot_general(fold, high, minor, preferred_element_type=F32)
        rows = rows + lax.dot_general(fold, low, minor, preferred_element_type=F32)
        firsts = [of32((cp * 2 + n) * 128 + t * 32) for n in range(2)]
        gate = jnp.concatenate([g_s[j, pl.ds(first, 32), :] for first in firsts], axis=0).astype(F32)
        gated = (rows / (1.0 + jnp.exp(-gate))).astype(BF)
        upd = jnp.dot(gated, wo_ref[...], preferred_element_type=F32)
        for n, first in enumerate(firsts):
            x = xs[(cp * 2 + n) * 2 + t // 2, j, pl.ds(of32(lax.rem(t, 2) * 32), 32), :]
            u_s[j, pl.ds(first, 32), :] = (x.astype(F32) + upd[n * 32 : n * 32 + 32]).astype(BF)

    def prologue():
        highest = None
        qm = queries(0, 0, 0)
        for kb in range(4):
            highest = score_block(0, 0, 0, 0, qm, kb, highest)
        m_s[0] = highest

    def task(f, b):
        t, cp, j = split(f)
        t2, cp2, j2 = split(jnp.minimum(f + 1, 127))
        t0, cp0, j0 = split(jnp.maximum(f - 1, 0))
        qm = queries(t2, cp2, j2)
        m = jnp.max(m_s[b], axis=0, keepdims=True)
        acc = None
        highest = None
        for kb in range(4):
            e = jnp.exp2((s_s[b, kb] - m) * LOG2E).astype(BF)
            highest = score_block(1 - b, t2, cp2, j2, qm, kb, highest)
            lhs = jnp.concatenate([v_s[j, :, kb * 256 : kb * 256 + 256], ones], axis=0)
            r = jnp.dot(lhs, e, preferred_element_type=F32)
            acc = r if acc is None else acc + r
            if kb == 1:
                finish(t0, cp0, j0, acc_s[1 - b])
        m_s[1 - b] = highest
        acc_s[b] = acc

    own = pltpu.make_async_copy(pair_ref.at[row], xs.at[row], osem)
    own.start()
    gather_step(0, 0)
    for n in range(1, 8):
        for d in range(3 * n - 3, min(3 * n, 15)):
            a2a(d).start()
        gather_step(n, 0)
        if n in (2, 4, 6):
            gather_step(n // 2 - 1, 1)
    own.wait()
    for n in range(15):
        a2a(n).wait()

    def prepare(j, _):
        for n, (chunk, step) in PREPARE.items():
            @pl.when(j == n)
            def _():
                gather_step(step, chunk)

        project(j)
        return 0

    lax.fori_loop(0, 8, prepare, 0)

    def chunk(t, _):
        def half(hh, _):
            for (tt, n), (later, step) in ATTEND.items():
                @pl.when(jnp.logical_and(hh == n, t == tt))
                def _():
                    gather_step(step, later)

            @pl.when(jnp.logical_and(hh == 1, t > 0))
            def _():
                exit_first(t - 1)

            @pl.when(jnp.logical_and(hh == 4, t > 0))
            def _():
                exit_second(t - 1)

            def two(i, _):
                task(t * 32 + hh * 4 + i * 2, 0)
                task(t * 32 + hh * 4 + i * 2 + 1, 1)
                return 0

            lax.fori_loop(0, 2, two, 0)
            return 0

        lax.fori_loop(0, 8, half, 0)
        return 0

    prologue()
    acc_s[1] = jnp.ones((144, 256), F32)
    lax.fori_loop(0, 4, chunk, 0)
    finish(3, 3, 7, acc_s[1])
    exit_first(3)
    exit_second(3)

    def drain(t, _):
        def one(c, _):
            either(
                2 * c + t // 2 == row, lambda: direct_local(c, t).wait(), lambda: direct_remote(c, t).wait_send()
            )
            return 0

        lax.fori_loop(0, 8, one, 0)
        for zz in range(2):
            for delta in (1, 2, 3):
                hop(delta, zz, t).wait_send()
            for n in range(4):
                here, rem, loc = mirror(n, zz, t)
                either(here, loc.wait, rem.wait_send)

        def arrived(s, _):
            @pl.when(jnp.logical_or(src_row0 + s != row, src_zh != zh))
            def _():
                mirror_arrival(s, t).wait_recv()

            return 0

        lax.fori_loop(0, 8, arrived, 0)
        return 0

    lax.fori_loop(0, 4, drain, 0)

    def landed(s, _):
        @pl.when(s != row)
        def _():
            for tt in range(2):
                direct_arrival(s, tt).wait_recv()

        return 0

    lax.fori_loop(0, 16, landed, 0)


def main(pair, bias, wa, wo):
    any_spec = pl.BlockSpec(memory_space=pl.ANY)
    vmem = pl.BlockSpec(memory_space=pltpu.VMEM)
    dma = pltpu.SemaphoreType.DMA
    return pl.pallas_call(
        main_kernel,
        out_shape=(jax.ShapeDtypeStruct((16, 8, 64, 128), BF), jax.ShapeDtypeStruct((8, 8, 128, 128), BF)),
        in_specs=[any_spec, vmem, vmem, vmem],
        out_specs=(any_spec,) * 2,
        scratch_shapes=[pltpu.VMEM((16, 8, 64, 128), BF)]
        + [pltpu.VMEM((4, 2, 4, 4, 4, n, 128), F32) for _, n in ROWS]
        + [
            pltpu.VMEM((8, 1024, 128), BF),
            pltpu.VMEM((8, 1024, 128), BF),
            pltpu.VMEM((8, 128, 1024), BF),
            pltpu.VMEM((8, 1024, 128), BF),
            pltpu.VMEM((2, 4, 256, 256), F32),
            pltpu.VMEM((2, 8, 256), F32),
            pltpu.VMEM((2, 144, 256), F32),
            pltpu.VMEM((8, 1024, 128), BF),
            pltpu.VMEM((4, 3, 2, 8, 32, 128), BF),
            dma((15,)), dma((15,)), dma,
            dma((4, 36)), dma((4, 36)), dma((4, 3)), dma((4, 3)), dma((4, 3)),
            dma((4, 8)), dma((2, 16)), dma((4, 3, 2)), dma((4, 3, 2)), dma((4, 4, 2)), dma((4, 8)), dma((2, 4)),
        ],
        compiler_params=pltpu.CompilerParams(collective_id=1, has_side_effects=True, vmem_limit_bytes=60 << 20),
        name="main",
    )(pair, bias, wa, wo)


def logits_kernel(d_ref, m_ref, wp_ref, we_ref, o_ref, flat):
    step = pl.program_id(0)

    @pl.when(step == 0)
    def _():
        def widen(g, _):
            for j in range(8):
                at = pl.multiple_of((g * 8 + j) * 64, 64)
                flat[pl.ds(at, 64), :] = d_ref[g, j].astype(F32)
            return 0

        lax.fori_loop(0, 16, widen, 0)

    for a in range(8):
        u = flat[pl.ds(step * 8 + a, 128, stride=64), :]
        sym = u + m_ref[a].astype(F32)
        pae = jnp.dot(layer_norm(u), wp_ref[...], preferred_element_type=F32)
        pde = jnp.dot(layer_norm(sym), we_ref[...], preferred_element_type=F32)
        o_ref[a] = pae + pde


def logits(d, m, wp, we):
    return pl.pallas_call(
        logits_kernel,
        grid=(8,),
        out_shape=jax.ShapeDtypeStruct((64, 128, 128), F32),
        in_specs=[
            pl.BlockSpec((16, 8, 64, 128), lambda t: (0, 0, 0, 0)),
            pl.BlockSpec((8, 128, 128), lambda t: (t, 0, 0)),
            pl.BlockSpec((128, 128), lambda t: (0, 0)),
            pl.BlockSpec((128, 128), lambda t: (0, 0)),
        ],
        out_specs=pl.BlockSpec((8, 128, 128), lambda t: (t, 0, 0)),
        scratch_shapes=[pltpu.VMEM((8192, 128), F32)],
        compiler_params=pltpu.CompilerParams(vmem_limit_bytes=40 << 20),
        name="logits",
    )(d, m, wp, we)


def per_device(z_trunk, coords, token_mask, w_dist, w_attn, w_bias, w_out, w_pae, w_pde):
    device = lax.axis_index("row") * 8 + lax.axis_index("col")
    info = jnp.concatenate([coords, token_mask[None]], axis=0).astype(F32)
    sub = jnp.pad(info.T, ((0, 0), (0, 124)))
    lane = jnp.arange(128, dtype=jnp.int32)[None, :] // 8 == lax.rem(device, 16)
    lane = jnp.where(lane, jnp.tile(info, (2, 16)), 0.0)
    wd = jnp.pad(w_dist, ((0, 1), (0, 0)))
    wb = jnp.pad(w_bias.T, ((0, 4), (0, 0)))
    pair, bias = embed(z_trunk, sub, lane, wd, wb)
    direct, mirror = main(pair, bias, w_attn, w_out)
    wp = jnp.pad(w_pae, ((0, 0), (0, 64)))
    we = jnp.pad(w_pde, ((0, 0), (64, 0)))
    return logits(direct, mirror.reshape(64, 128, 128), wp, we)


def solution(mesh):
    in_specs = (P("row", "col", None), P(None, ("row", "col")), P(("row", "col")), P(), P(), P(), P(), P(), P())
    return jax.shard_map(
        per_device, mesh=mesh, in_specs=in_specs, out_specs=P("row", "col", None), check_vma=False
    )
```

```python
import functools

import jax
import jax.numpy as jnp
from jax import lax
from jax.experimental import pallas as pl
from jax.experimental.pallas import tpu as pltpu
from jax.sharding import PartitionSpec as P

MESH = pl.DeviceIdType.MESH
BF = jnp.bfloat16
F32 = jnp.float32
LOG2E = 1.4426950408889634
ORDERS = (("y", "z", "x"), ("z", "x", "y"), ("x", "y", "z"))
ROWS = ((0, 24), (24, 24), (48, 16))
SPREAD = (
    (1, 0, 0), (3, 0, 0), (0, 1, 0), (2, 0, 0), (1, 1, 0), (3, 1, 0), (0, 0, 1), (2, 1, 0),
    (1, 0, 1), (3, 0, 1), (0, 1, 1), (2, 0, 1), (1, 1, 1), (3, 1, 1), (2, 1, 1),
)
PREPARE = {0: (1, 3), 1: (2, 0), 5: (0, 5), 7: (2, 1)}
ATTEND = {
    (0, 0): (1, 4), (0, 2): (2, 2), (0, 3): (3, 0), (0, 4): (1, 5), (0, 5): (2, 3), (0, 6): (3, 1),
    (1, 0): (2, 4), (1, 1): (3, 2), (1, 3): (2, 5), (1, 4): (3, 3), (1, 7): (3, 4), (2, 2): (3, 5),
}


def layer_norm(values):
    widened = values.astype(F32)
    average = jnp.mean(widened, axis=-1, keepdims=True)
    centred = widened - average
    variance = jnp.mean(centred * centred, axis=-1, keepdims=True)
    return (centred * lax.rsqrt(variance + 1e-05)).astype(BF)


def remote(src, dst, send, recv, device):
    return pltpu.make_async_remote_copy(
        src_ref=src, dst_ref=dst, send_sem=send, recv_sem=recv, device_id=device, device_id_type=MESH
    )


def embed_kernel(z_ref, sub_ref, lane_ref, wd_ref, wb_ref, pair_ref, bias_ref,
                 rs, rl, flat, s_send, s_recv, l_send, l_recv):
    row = lax.axis_index("row")
    col = lax.axis_index("col")
    slot = lax.rem(row, 2) * 8 + col
    target = row // 2
    barrier = pltpu.get_barrier_semaphore()

    def greet_row(d, _):
        pl.semaphore_signal(barrier, inc=1, device_id=(row, lax.rem(col + d, 8)), device_id_type=MESH)
        return 0

    lax.fori_loop(1, 8, greet_row, 0)

    def greet_source(s, _):
        src_row = 2 * col + s // 8
        src_col = lax.rem(s, 8)

        @pl.when(jnp.logical_or(src_row != row, src_col != col))
        def _():
            pl.semaphore_signal(barrier, inc=1, device_id=(src_row, src_col), device_id_type=MESH)

        return 0

    lax.fori_loop(0, 16, greet_source, 0)

    @pl.when(target == col)
    def _():
        pl.semaphore_wait(barrier, 22)

    @pl.when(target != col)
    def _():
        pl.semaphore_wait(barrier, 23)

    def row_copy(d):
        to = lax.rem(col + d, 8)
        return remote(sub_ref, rs.at[col], s_send.at[d - 1], s_recv.at[d - 1], (row, to))

    def lane_copy(r):
        return remote(lane_ref, rl.at[slot], l_send.at[r], l_recv.at[slot], (r, target))

    def lane_arrival(s):
        return remote(lane_ref, rl.at[s], l_send.at[s], l_recv.at[s], (2 * col + s // 8, lax.rem(s, 8)))

    def start_row(d, _):
        row_copy(d).start()
        return 0

    lax.fori_loop(1, 8, start_row, 0)

    def start_lane(r, _):
        @pl.when(jnp.logical_or(r != row, target != col))
        def _():
            lane_copy(r).start()

        return 0

    lax.fori_loop(0, 16, start_lane, 0)
    rs[col] = sub_ref[...]

    @pl.when(target == col)
    def _():
        rl[slot] = lane_ref[...]

    def wait_row(d, _):
        row_copy(d).wait()
        return 0

    lax.fori_loop(1, 8, wait_row, 0)

    def wait_lane(r, _):
        @pl.when(jnp.logical_or(r != row, target != col))
        def _():
            lane_copy(r).wait_send()

        @pl.when(jnp.logical_or(2 * col + r // 8 != row, lax.rem(r, 8) != col))
        def _():
            lane_arrival(r).wait_recv()

        return 0

    lax.fori_loop(0, 16, wait_lane, 0)

    lanes = jnp.sum(rl[...], axis=0)
    turned = jnp.concatenate([lanes] * 16, axis=0).T
    cx, cy, cz = (jnp.broadcast_to(turned[:, n : n + 1], (128, 128)) for n in range(3))
    edge = lax.broadcasted_iota(jnp.int32, (1, 128), 1)
    upper_edge = 27 + 4 * edge
    lower_edge = 23 + 4 * edge
    big = jnp.int32(1 << 20)
    lower = jnp.where(edge == 0, -1, jnp.where(edge >= 39, big, lower_edge * lower_edge)).astype(F32)
    upper = jnp.where(edge >= 38, big, upper_edge * upper_edge).astype(F32)
    head = lax.broadcasted_iota(jnp.int32, (8, 128), 1) // 32

    def eight(t, _):
        own = rs[t]
        key_bias = (own[:, 3:4] - 1.0) * 30000.0
        hots = []
        for a in range(8):
            dx = cx - own[a : a + 1, 0:1]
            dy = cy - own[a : a + 1, 1:2]
            dz = cz - own[a : a + 1, 2:3]
            squared = dx * dx + dy * dy + dz * dz
            hots.append(jnp.where(jnp.logical_and(squared > lower, squared <= upper), 1.0, 0.0).astype(BF))
        added = jnp.dot(jnp.concatenate(hots, axis=0), wd_ref[...], preferred_element_type=F32)
        start = pl.multiple_of(t * 8, 8)
        z = z_ref[pl.ds(start, 8)].reshape(1024, 128).astype(F32)
        pair = (z + added).astype(BF)
        wide = pair.astype(F32)
        for a in range(8):
            flat[pl.ds(start + a, 128, stride=64), :] = wide[a * 128 : a * 128 + 128]
        normed = layer_norm(pair)
        b = lax.dot_general(wb_ref[...], normed, (((1,), (1,)), ((), ())), preferred_element_type=F32)
        by_head = [
            jnp.concatenate([b[h : h + 1, a * 128 : a * 128 + 128] for a in range(8)], axis=0) + key_bias
            for h in range(4)
        ]
        for c in range(4):
            moved = [pltpu.roll(by_head[h], (32 * h - 32 * c) % 128, 1) for h in range(4)]
            block = moved[3]
            for h in (2, 1, 0):
                block = jnp.where(head == h, moved[h], block)
            bias_ref[c, pl.ds(start, 8), :] = block
        return 0

    lax.fori_loop(0, 8, eight, 0, unroll=4)

    def out(g, _):
        for j in range(8):
            at = pl.multiple_of((g * 8 + j) * 64, 64)
            pair_ref[g, j] = flat[pl.ds(at, 64), :].astype(BF)
        return 0

    lax.fori_loop(0, 16, out, 0)


def embed(z, sub, lane, wd, wb):
    return pl.pallas_call(
        embed_kernel,
        out_shape=(
            jax.ShapeDtypeStruct((16, 8, 64, 128), BF),
            jax.ShapeDtypeStruct((4, 64, 128), F32),
        ),
        in_specs=[pl.BlockSpec(memory_space=pltpu.VMEM)] * 5,
        out_specs=(pl.BlockSpec(memory_space=pltpu.VMEM),) * 2,
        scratch_shapes=[
            pltpu.VMEM((8, 8, 128), F32),
            pltpu.VMEM((16, 8, 128), F32),
            pltpu.VMEM((8192, 128), F32),
            pltpu.SemaphoreType.DMA((7,)),
            pltpu.SemaphoreType.DMA((7,)),
            pltpu.SemaphoreType.DMA((16,)),
            pltpu.SemaphoreType.DMA((16,)),
        ],
        compiler_params=pltpu.CompilerParams(collective_id=0, has_side_effects=True, vmem_limit_bytes=40 << 20),
        name="embed",
    )(z, sub, lane, wd, wb)


def place():
    row = lax.axis_index("row")
    col = lax.axis_index("col")
    core = lax.rem(row, 2)
    at = {"x": lax.rem(col, 4), "y": row // 4, "z": (col // 4) * 2 + lax.rem(row // 2, 2)}
    return row, col, core, at


def device_of(at, core):
    return (at["y"] * 4 + lax.rem(at["z"], 2) * 2 + core, (at["z"] // 2) * 4 + at["x"])


def beside(at, dim, delta):
    moved = dict(at)
    moved[dim] = lax.rem(at[dim] + delta + 4, 4)
    return moved


def of32(n):
    return pl.multiple_of(n, 32)


def main_kernel(pair_ref, bias_ref, wa_ref, wo_ref, d_ref, m_ref,
                xs, g0, g1, g2, q_s, k_s, v_s, g_s, s_s, m_s, acc_s, u_s, relay,
                asend, arecv, osem, send, recv, lsem, psend, precv,
                dsend, drecv, rsend, rrecv, msend, mrecv, hsem):
    row, col, core, at = place()
    gs = (g0, g1, g2)
    zh = col // 4
    yh = row // 8
    partner = device_of(at, 1 - core)
    looped = jnp.logical_and(yh == zh, core == yh)
    src_row0 = core * 8
    src_zh = yh
    slot = lax.rem(row, 8)
    barrier = pltpu.get_barrier_semaphore()

    def signal(device):
        pl.semaphore_signal(barrier, inc=1, device_id=device, device_id_type=MESH)

    def greet(d, _):
        signal((lax.rem(row + d, 16), col))
        return 0

    lax.fori_loop(1, 16, greet, 0)
    for dim in ("x", "y", "z"):
        for delta in (1, -1):
            signal(device_of(beside(at, dim, delta), core))
    signal(device_of(beside(at, "x", 2), core))
    signal(device_of(beside(at, "z", 2), core))

    def greet_relay(s, _):
        @pl.when(jnp.logical_or(src_row0 + s != row, src_zh != zh))
        def _():
            signal((src_row0 + s, src_zh * 4 + at["x"]))

        return 0

    lax.fori_loop(0, 8, greet_relay, 0)

    @pl.when(looped)
    def _():
        pl.semaphore_wait(barrier, 30)

    @pl.when(jnp.logical_not(looped))
    def _():
        pl.semaphore_wait(barrier, 31)

    def a2a(n):
        dy, dz, dc = SPREAD[n]
        to = lax.rem(at["y"] + dy, 4) * 4 + lax.rem(lax.rem(row // 2, 2) + dz, 2) * 2 + lax.rem(core + dc, 2)
        return remote(pair_ref.at[to], xs.at[row], asend.at[n], arecv.at[n], (to, col))

    def gather_copy(stage, p, k, t):
        dims = ORDERS[p]
        first, count = ROWS[p]
        g = gs[p]
        delta = (1, -1, 2)[k] if stage < 2 else (1, -1)[k % 2]
        a = [at[d] for d in dims]
        if stage == 2 and k >= 2:
            a[stage] = lax.rem(a[stage] - delta + 4, 4)
        a1, a2, a3 = a
        if stage == 0:
            src = bias_ref.at[t, pl.ds(first, count), :]
            dst = g.at[t, core, a3, a2, a1]
        else:
            src = g.at[t, core, a3, a2] if stage == 1 else g.at[t, core, a3]
            if stage == 2 and k >= 2:
                src = src.at[pl.ds(2 * (k % 2), 2)]
            dst = src
        n = p * 10 + stage * 3 + k
        return remote(src, dst, send.at[t, n], recv.at[t, n], device_of(beside(at, dims[stage], delta), core))

    def keep(p, t):
        a1, a2, a3 = (at[d] for d in ORDERS[p])
        first, count = ROWS[p]
        return pltpu.make_async_copy(
            bias_ref.at[t, pl.ds(first, count), :], gs[p].at[t, core, a3, a2, a1], lsem.at[t, p]
        )

    def share(p, k, t):
        a3 = lax.rem(at[ORDERS[p][2]] + (0, 3, 1, 2)[k], 4)
        plane = gs[p].at[t, core, a3]
        return remote(plane, plane, psend.at[t, p * 4 + k], precv.at[t, p * 4 + k], partner)

    def gather_step(n, t):
        parts = range(3)
        if n == 0:
            for p in parts:
                keep(p, t).start()
                for k in range(3):
                    gather_copy(0, p, k, t).start()
        elif n in (1, 2):
            for p in parts:
                if n == 1:
                    keep(p, t).wait()
                for k in range(3):
                    gather_copy(n - 1, p, k, t).wait_recv()
                for k in range(3 if n == 1 else 2):
                    gather_copy(n, p, k, t).start()
            if n == 2:
                for p in parts:
                    share(p, 0, t).start()
        elif n == 3:
            for p in parts:
                for k in (0, 1):
                    gather_copy(2, p, k, t).wait_recv()
                    gather_copy(2, p, k + 2, t).start()
            for p in parts:
                for k in (0, 1):
                    share(p, k + 1, t).start()
        elif n == 4:
            for p in parts:
                for k in (2, 3):
                    gather_copy(2, p, k, t).wait_recv()
                share(p, 3, t).start()
        else:
            for p in parts:
                for k in range(4):
                    share(p, k, t).wait()
                for stage in range(3):
                    for k in range(3 if stage < 2 else 4):
                        gather_copy(stage, p, k, t).wait_send()

    def direct(c, t):
        to = 2 * c + t // 2
        return (
            to,
            u_s.at[:, pl.ds(of32(c * 128 + t * 32), 32), :],
            d_ref.at[row, :, pl.ds(of32(lax.rem(t, 2) * 32), 32), :],
            dsend.at[t, c],
            drecv.at[lax.rem(t, 2), row],
        )

    def direct_remote(c, t):
        to, src, dst, s1, s2 = direct(c, t)
        return remote(src, dst, s1, s2, (to, col))

    def direct_local(c, t):
        to, src, dst, s1, s2 = direct(c, t)
        return pltpu.make_async_copy(src, dst, hsem.at[0, lax.rem(t, 2)])

    def direct_arrival(s, tt):
        return remote(
            u_s.at[:, pl.ds(0, 32), :], d_ref.at[s, :, pl.ds(of32(tt * 32), 32), :],
            dsend.at[0, 0], drecv.at[tt, s], (s, col),
        )

    def hop(delta, zz, t):
        x2 = lax.rem(at["x"] + delta, 4)
        c = zz * 4 + x2
        return remote(
            u_s.at[:, pl.ds(of32(c * 128 + t * 32), 32), :], relay.at[t, 3 - delta, zz],
            rsend.at[t, delta - 1, zz], rrecv.at[t, 3 - delta, zz], device_of(beside(at, "x", delta), core),
        )

    def hop_arrival(n, zz, t):
        return remote(
            u_s.at[:, pl.ds(0, 32), :], relay.at[t, n, zz],
            rsend.at[t, 2 - n, zz], rrecv.at[t, n, zz], device_of(beside(at, "x", n + 1), core),
        )

    def mirror(n, zz, t):
        sx = lax.rem(at["x"] + n, 4)
        to_row = 2 * (4 * zh + sx) + yh
        c = zz * 4 + at["x"]
        if n == 0:
            src = u_s.at[:, pl.ds(of32(c * 128 + t * 32), 32), :]
        else:
            src = relay.at[t, n - 1, zz]
        dst = m_ref.at[slot, :, pl.ds(of32(t * 32), 32), :]
        here = jnp.logical_and(to_row == row, zz == zh)
        rem = remote(src, dst, msend.at[t, n, zz], mrecv.at[t, slot], (to_row, c))
        loc = pltpu.make_async_copy(src, dst, hsem.at[1, t])
        return here, rem, loc

    def mirror_arrival(s, t):
        return remote(
            u_s.at[:, pl.ds(0, 32), :], m_ref.at[s, :, pl.ds(of32(t * 32), 32), :],
            msend.at[t, 0, 0], mrecv.at[t, s], (src_row0 + s, src_zh * 4 + at["x"]),
        )

    def either(here, if_here, otherwise):
        @pl.when(here)
        def _():
            if_here()

        @pl.when(jnp.logical_not(here))
        def _():
            otherwise()

    def exit_first(t, zz):
        for delta in (1, 2, 3):
            hop(delta, zz, t).start()
        here, rem, loc = mirror(0, zz, t)
        either(here, loc.start, rem.start)

        def go(n, _):
            c = zz * 4 + lax.rem(at["x"] + n, 4)
            either(
                2 * c + t // 2 == row, lambda: direct_local(c, t).start(), lambda: direct_remote(c, t).start()
            )
            return 0

        lax.fori_loop(0, 4, go, 0)

    def exit_second(t, zz):
        for n in (1, 2, 3):
            hop_arrival(n - 1, zz, t).wait_recv()
            here, rem, loc = mirror(n, zz, t)
            either(here, loc.start, rem.start)

    def project(j):
        p = jnp.dot(layer_norm(xs[:, j].reshape(1024, 128)), wa_ref[...], preferred_element_type=F32)
        q_s[j] = (p[:, :128] * (32**-0.5)).astype(BF)
        k_s[j] = p[:, 128:256].astype(BF)
        v_s[j] = p[:, 256:384].astype(BF).T
        g_s[j] = p[:, 384:].astype(BF)

    head_of_lane = lax.broadcasted_iota(jnp.int32, (32, 128), 1) // 32
    ones = jnp.ones((16, 256), BF)

    def bias_block(t, cp, kb, n):
        parts = []
        for zl in range(2):
            for cc in range(2):
                for p in range(3):
                    where = {"x": 2 * lax.rem(cp, 2) + n, "y": kb, "z": 2 * (cp // 2) + zl}
                    d1, d2, d3 = ORDERS[p]
                    parts.append(gs[p][t, cc, where[d3], where[d2], where[d1]])
        return jnp.concatenate(parts, axis=0)

    diagonal = lax.broadcasted_iota(jnp.int32, (128, 256), 0) // 32 == lax.rem(
        lax.broadcasted_iota(jnp.int32, (128, 256), 1) // 32, 4
    )
    fold_row = lax.broadcasted_iota(jnp.int32, (64, 256), 0)
    fold_lane = lax.broadcasted_iota(jnp.int32, (64, 256), 1)
    fold = jnp.where(
        jnp.logical_and(fold_row // 32 == fold_lane // 128, lax.rem(fold_row, 32) == lax.rem(fold_lane, 32)), 1.0, 0.0
    ).astype(BF)
    minor = (((1,), (1,)), ((), ()))

    def split(f):
        return f // 32, lax.rem(f, 32) // 8, lax.rem(f, 8)

    def queries(t, cp, j):
        parts = []
        for n in range(2):
            q = q_s[j, pl.ds(of32((cp * 2 + n) * 128 + t * 32), 32), :]
            for h in range(4):
                parts.append(jnp.where(head_of_lane == h, q, jnp.zeros_like(q)))
        return jnp.concatenate(parts, axis=0)

    def score(t, cp, j, qm, kb):
        s = lax.dot_general(k_s[j, pl.ds(kb * 256, 256), :], qm, minor, preferred_element_type=F32)
        return s + jnp.concatenate([bias_block(t, cp, kb, 0), bias_block(t, cp, kb, 1)], axis=1)

    def score_block(b, t, cp, j, qm, kb, highest):
        s = score(t, cp, j, qm, kb)
        s_s[b, kb] = s
        here = jnp.max(s.reshape(32, 8, 256), axis=0)
        return here if highest is None else jnp.maximum(highest, here)

    def finish(t, cp, j, acc):
        att = jnp.where(diagonal, acc[:128] * (1.0 / acc[128:129]), 0.0)
        high = att.astype(BF)
        low = (att - high.astype(F32)).astype(BF)
        rows = lax.dot_general(fold, high, minor, preferred_element_type=F32)
        rows = rows + lax.dot_general(fold, low, minor, preferred_element_type=F32)
        firsts = [of32((cp * 2 + n) * 128 + t * 32) for n in range(2)]
        gate = jnp.concatenate([g_s[j, pl.ds(first, 32), :] for first in firsts], axis=0).astype(F32)
        gated = (rows / (1.0 + jnp.exp(-gate))).astype(BF)
        upd = jnp.dot(gated, wo_ref[...], preferred_element_type=F32)
        for n, first in enumerate(firsts):
            x = xs[(cp * 2 + n) * 2 + t // 2, j, pl.ds(of32(lax.rem(t, 2) * 32), 32), :]
            u_s[j, pl.ds(first, 32), :] = (x.astype(F32) + upd[n * 32 : n * 32 + 32]).astype(BF)

    def prologue():
        highest = None
        qm = queries(0, 0, 0)
        for kb in range(4):
            highest = score_block(0, 0, 0, 0, qm, kb, highest)
        m_s[0] = highest

    def task(f, b):
        t, cp, j = split(f)
        t2, cp2, j2 = split(jnp.minimum(f + 1, 127))
        t0, cp0, j0 = split(jnp.maximum(f - 1, 0))
        qm = queries(t2, cp2, j2)
        m = jnp.max(m_s[b], axis=0, keepdims=True)
        acc = None
        highest = None
        for kb in range(4):
            e = jnp.exp2((s_s[b, kb] - m) * LOG2E).astype(BF)
            highest = score_block(1 - b, t2, cp2, j2, qm, kb, highest)
            lhs = jnp.concatenate([v_s[j, :, kb * 256 : kb * 256 + 256], ones], axis=0)
            r = jnp.dot(lhs, e, preferred_element_type=F32)
            acc = r if acc is None else acc + r
            if kb == 1:
                finish(t0, cp0, j0, acc_s[1 - b])
        m_s[1 - b] = highest
        acc_s[b] = acc

    own = pltpu.make_async_copy(pair_ref.at[row], xs.at[row], osem)
    own.start()
    gather_step(0, 0)
    gather_step(0, 1)
    for n in range(1, 5):
        for d in range(4 * n - 4, min(4 * n, 15)):
            a2a(d).start()
        gather_step(n, 0)
        if n < 3:
            gather_step(n, 1)
    own.wait()
    for n in range(15):
        a2a(n).wait()

    def prepare(j, _):
        for n, (chunk, step) in PREPARE.items():
            @pl.when(j == n)
            def _():
                gather_step(step, chunk)

        project(j)
        return 0

    lax.fori_loop(0, 8, prepare, 0)

    def chunk(t, _):
        def half(hh, _):
            for (tt, n), (later, step) in ATTEND.items():
                @pl.when(jnp.logical_and(hh == n, t == tt))
                def _():
                    gather_step(step, later)

            @pl.when(jnp.logical_and(hh == 1, t > 0))
            def _():
                exit_first(t - 1, 1)

            @pl.when(jnp.logical_and(hh == 0, t > 0))
            def _():
                exit_second(t - 1, 0)

            @pl.when(jnp.logical_and(hh == 4, t > 0))
            def _():
                exit_second(t - 1, 1)

            @pl.when(hh == 5)
            def _():
                exit_first(t, 0)

            def two(i, _):
                task(t * 32 + hh * 4 + i * 2, 0)
                task(t * 32 + hh * 4 + i * 2 + 1, 1)
                return 0

            lax.fori_loop(0, 2, two, 0)
            return 0

        lax.fori_loop(0, 8, half, 0)
        return 0

    prologue()
    acc_s[1] = jnp.ones((144, 256), F32)
    lax.fori_loop(0, 4, chunk, 0)
    finish(3, 3, 7, acc_s[1])
    exit_first(3, 1)
    exit_second(3, 0)
    exit_second(3, 1)

    def drain(t, _):
        def one(c, _):
            either(
                2 * c + t // 2 == row, lambda: direct_local(c, t).wait(), lambda: direct_remote(c, t).wait_send()
            )
            return 0

        lax.fori_loop(0, 8, one, 0)
        for zz in range(2):
            for delta in (1, 2, 3):
                hop(delta, zz, t).wait_send()
            for n in range(4):
                here, rem, loc = mirror(n, zz, t)
                either(here, loc.wait, rem.wait_send)

        def arrived(s, _):
            @pl.when(jnp.logical_or(src_row0 + s != row, src_zh != zh))
            def _():
                mirror_arrival(s, t).wait_recv()

            return 0

        lax.fori_loop(0, 8, arrived, 0)
        return 0

    lax.fori_loop(0, 4, drain, 0)

    def landed(s, _):
        @pl.when(s != row)
        def _():
            for tt in range(2):
                direct_arrival(s, tt).wait_recv()

        return 0

    lax.fori_loop(0, 16, landed, 0)


def main(pair, bias, wa, wo):
    any_spec = pl.BlockSpec(memory_space=pl.ANY)
    vmem = pl.BlockSpec(memory_space=pltpu.VMEM)
    dma = pltpu.SemaphoreType.DMA
    return pl.pallas_call(
        main_kernel,
        out_shape=(jax.ShapeDtypeStruct((16, 8, 64, 128), BF), jax.ShapeDtypeStruct((8, 8, 128, 128), BF)),
        in_specs=[any_spec, vmem, vmem, vmem],
        out_specs=(any_spec,) * 2,
        scratch_shapes=[pltpu.VMEM((16, 8, 64, 128), BF)]
        + [pltpu.VMEM((4, 2, 4, 4, 4, n, 128), F32) for _, n in ROWS]
        + [
            pltpu.VMEM((8, 1024, 128), BF),
            pltpu.VMEM((8, 1024, 128), BF),
            pltpu.VMEM((8, 128, 1024), BF),
            pltpu.VMEM((8, 1024, 128), BF),
            pltpu.VMEM((2, 4, 256, 256), F32),
            pltpu.VMEM((2, 8, 256), F32),
            pltpu.VMEM((2, 144, 256), F32),
            pltpu.VMEM((8, 1024, 128), BF),
            pltpu.VMEM((4, 3, 2, 8, 32, 128), BF),
            dma((15,)), dma((15,)), dma,
            dma((4, 30)), dma((4, 30)), dma((4, 3)), dma((4, 12)), dma((4, 12)),
            dma((4, 8)), dma((2, 16)), dma((4, 3, 2)), dma((4, 3, 2)), dma((4, 4, 2)), dma((4, 8)), dma((2, 4)),
        ],
        compiler_params=pltpu.CompilerParams(collective_id=1, has_side_effects=True, vmem_limit_bytes=60 << 20),
        name="main",
    )(pair, bias, wa, wo)


def logits_kernel(d_ref, m_ref, wp_ref, we_ref, o_ref, flat):
    step = pl.program_id(0)

    @pl.when(step == 0)
    def _():
        def widen(g, _):
            for j in range(8):
                at = pl.multiple_of((g * 8 + j) * 64, 64)
                flat[pl.ds(at, 64), :] = d_ref[g, j].astype(F32)
            return 0

        lax.fori_loop(0, 16, widen, 0)

    for a in range(8):
        u = flat[pl.ds(step * 8 + a, 128, stride=64), :]
        sym = u + m_ref[a].astype(F32)
        pae = jnp.dot(layer_norm(u), wp_ref[...], preferred_element_type=F32)
        pde = jnp.dot(layer_norm(sym), we_ref[...], preferred_element_type=F32)
        o_ref[a] = pae + pde


def logits(d, m, wp, we):
    return pl.pallas_call(
        logits_kernel,
        grid=(8,),
        out_shape=jax.ShapeDtypeStruct((64, 128, 128), F32),
        in_specs=[
            pl.BlockSpec((16, 8, 64, 128), lambda t: (0, 0, 0, 0)),
            pl.BlockSpec((8, 128, 128), lambda t: (t, 0, 0)),
            pl.BlockSpec((128, 128), lambda t: (0, 0)),
            pl.BlockSpec((128, 128), lambda t: (0, 0)),
        ],
        out_specs=pl.BlockSpec((8, 128, 128), lambda t: (t, 0, 0)),
        scratch_shapes=[pltpu.VMEM((8192, 128), F32)],
        compiler_params=pltpu.CompilerParams(vmem_limit_bytes=40 << 20),
        name="logits",
    )(d, m, wp, we)


def per_device(z_trunk, coords, token_mask, w_dist, w_attn, w_bias, w_out, w_pae, w_pde):
    device = lax.axis_index("row") * 8 + lax.axis_index("col")
    info = jnp.concatenate([coords, token_mask[None]], axis=0).astype(F32)
    sub = jnp.pad(info.T, ((0, 0), (0, 124)))
    lane = jnp.arange(128, dtype=jnp.int32)[None, :] // 8 == lax.rem(device, 16)
    lane = jnp.where(lane, jnp.tile(info, (2, 16)), 0.0)
    wd = jnp.pad(w_dist, ((0, 89), (0, 0)))
    wb = jnp.pad(w_bias.T, ((0, 4), (0, 0)))
    pair, bias = embed(z_trunk, sub, lane, wd, wb)
    direct, mirror = main(pair, bias, w_attn, w_out)
    wp = jnp.pad(w_pae, ((0, 0), (0, 64)))
    we = jnp.pad(w_pde, ((0, 0), (64, 0)))
    return logits(direct, mirror.reshape(64, 128, 128), wp, we)


def solution(mesh):
    in_specs = (P("row", "col", None), P(None, ("row", "col")), P(("row", "col")), P(), P(), P(), P(), P(), P())
    return jax.shard_map(
        per_device, mesh=mesh, in_specs=in_specs, out_specs=P("row", "col", None), check_vma=False
    )
```

```python
import functools

import jax
import jax.numpy as jnp
from jax import lax
from jax.experimental import pallas as pl
from jax.experimental.pallas import tpu as pltpu
from jax.sharding import PartitionSpec as P

MESH = pl.DeviceIdType.MESH
BF = jnp.bfloat16
F32 = jnp.float32
LOG2E = 1.4426950408889634
ORDERS = (("y", "z", "x"), ("z", "x", "y"), ("x", "y", "z"))
ROWS = ((0, 24), (24, 24), (48, 16))
SPREAD = (
    (1, 0, 0), (3, 0, 0), (0, 1, 0), (2, 0, 0), (1, 1, 0), (3, 1, 0), (0, 0, 1), (2, 1, 0),
    (1, 0, 1), (3, 0, 1), (0, 1, 1), (2, 0, 1), (1, 1, 1), (3, 1, 1), (2, 1, 1),
)
PREPARE = {0: (1, 3), 1: (2, 0), 3: (0, 5)}
ATTEND = {
    (0, 0): (1, 4), (0, 1): (2, 1), (0, 2): (2, 2), (0, 3): (3, 0), (0, 4): (1, 5), (0, 5): (2, 3), (0, 6): (3, 1),
    (1, 0): (2, 4), (1, 1): (3, 2), (1, 3): (2, 5), (1, 4): (3, 3), (1, 7): (3, 4), (2, 2): (3, 5),
}


def layer_norm(values):
    widened = values.astype(F32)
    average = jnp.mean(widened, axis=-1, keepdims=True)
    centred = widened - average
    variance = jnp.mean(centred * centred, axis=-1, keepdims=True)
    return (centred * lax.rsqrt(variance + 1e-05)).astype(BF)


def remote(src, dst, send, recv, device):
    return pltpu.make_async_remote_copy(
        src_ref=src, dst_ref=dst, send_sem=send, recv_sem=recv, device_id=device, device_id_type=MESH
    )


def embed_kernel(z_hbm, coords_ref, mask_ref, wd_raw, wb_ref, pair_hbm, bias_ref,
                 z_ref, pair_s, wd_ref, info, sub_ref, lane_ref, rs, rl, flat,
                 s_send, s_recv, l_send, l_recv, z_sem, out_sem):
    load_z = pltpu.make_async_copy(z_hbm, z_ref, z_sem)
    load_z.start()
    row = lax.axis_index("row")
    col = lax.axis_index("col")
    slot = lax.rem(row, 2) * 8 + col
    target = row // 2
    info[...] = jnp.zeros((8, 128), F32)
    info[0:3, 0:8] = coords_ref[...].astype(F32)
    info[3:4, 0:8] = mask_ref[...].astype(F32)
    tokens = info[...]
    sub_ref[...] = jnp.concatenate([tokens] * 16, axis=0).T[0:8]
    lane_ref[...] = pltpu.roll(tokens, slot * 8, 1)
    wd_ref[...] = jnp.zeros((128, 128), BF)
    wd_ref[0:39] = wd_raw[...]
    barrier = pltpu.get_barrier_semaphore()

    def greet_row(d, _):
        pl.semaphore_signal(barrier, inc=1, device_id=(row, lax.rem(col + d, 8)), device_id_type=MESH)
        return 0

    lax.fori_loop(1, 8, greet_row, 0)

    def greet_source(s, _):
        src_row = 2 * col + s // 8
        src_col = lax.rem(s, 8)

        @pl.when(jnp.logical_or(src_row != row, src_col != col))
        def _():
            pl.semaphore_signal(barrier, inc=1, device_id=(src_row, src_col), device_id_type=MESH)

        return 0

    lax.fori_loop(0, 16, greet_source, 0)

    @pl.when(target == col)
    def _():
        pl.semaphore_wait(barrier, 22)

    @pl.when(target != col)
    def _():
        pl.semaphore_wait(barrier, 23)

    def row_copy(d):
        to = lax.rem(col + d, 8)
        return remote(sub_ref, rs.at[col], s_send.at[d - 1], s_recv.at[d - 1], (row, to))

    def lane_copy(r):
        return remote(lane_ref, rl.at[slot], l_send.at[r], l_recv.at[slot], (r, target))

    def lane_arrival(s):
        return remote(lane_ref, rl.at[s], l_send.at[s], l_recv.at[s], (2 * col + s // 8, lax.rem(s, 8)))

    def start_row(d, _):
        row_copy(d).start()
        return 0

    lax.fori_loop(1, 8, start_row, 0)

    def start_lane(r, _):
        @pl.when(jnp.logical_or(r != row, target != col))
        def _():
            lane_copy(r).start()

        return 0

    lax.fori_loop(0, 16, start_lane, 0)
    rs[col] = sub_ref[...]

    @pl.when(target == col)
    def _():
        rl[slot] = lane_ref[...]

    def wait_row(d, _):
        row_copy(d).wait()
        return 0

    lax.fori_loop(1, 8, wait_row, 0)

    def wait_lane(r, _):
        @pl.when(jnp.logical_or(r != row, target != col))
        def _():
            lane_copy(r).wait_send()

        @pl.when(jnp.logical_or(2 * col + r // 8 != row, lax.rem(r, 8) != col))
        def _():
            lane_arrival(r).wait_recv()

        return 0

    lax.fori_loop(0, 16, wait_lane, 0)

    lanes = jnp.sum(rl[...], axis=0)
    turned = jnp.concatenate([lanes] * 16, axis=0).T
    cx, cy, cz = (jnp.broadcast_to(turned[:, n : n + 1], (128, 128)) for n in range(3))
    edge = lax.broadcasted_iota(jnp.int32, (1, 128), 1)
    upper_edge = 27 + 4 * edge
    lower_edge = 23 + 4 * edge
    big = jnp.int32(1 << 20)
    lower = jnp.where(edge == 0, -1, jnp.where(edge >= 39, big, lower_edge * lower_edge)).astype(F32)
    upper = jnp.where(edge >= 38, big, upper_edge * upper_edge).astype(F32)
    head = lax.broadcasted_iota(jnp.int32, (8, 128), 1) // 32

    load_z.wait()

    def eight(t, _):
        own = rs[t]
        key_bias = (own[:, 3:4] - 1.0) * 30000.0
        hots = []
        for a in range(8):
            dx = cx - own[a : a + 1, 0:1]
            dy = cy - own[a : a + 1, 1:2]
            dz = cz - own[a : a + 1, 2:3]
            squared = dx * dx + dy * dy + dz * dz
            hots.append(jnp.where(jnp.logical_and(squared > lower, squared <= upper), 1.0, 0.0).astype(BF))
        added = jnp.dot(jnp.concatenate(hots, axis=0), wd_ref[...], preferred_element_type=F32)
        start = pl.multiple_of(t * 8, 8)
        z = z_ref[pl.ds(start, 8)].reshape(1024, 128).astype(F32)
        pair = (z + added).astype(BF)
        wide = pair.astype(F32)
        for a in range(8):
            flat[pl.ds(start + a, 128, stride=64), :] = wide[a * 128 : a * 128 + 128]
        normed = layer_norm(pair)
        b = lax.dot_general(wb_ref[...], normed, (((1,), (1,)), ((), ())), preferred_element_type=F32)
        by_head = [
            jnp.concatenate([b[h : h + 1, a * 128 : a * 128 + 128] for a in range(8)], axis=0) + key_bias
            for h in range(4)
        ]
        for c in range(4):
            moved = [pltpu.roll(by_head[h], (32 * h - 32 * c) % 128, 1) for h in range(4)]
            block = moved[3]
            for h in (2, 1, 0):
                block = jnp.where(head == h, moved[h], block)
            bias_ref[c, pl.ds(start, 8), :] = block
        return 0

    lax.fori_loop(0, 8, eight, 0, unroll=4)

    def out_copy(g):
        return pltpu.make_async_copy(pair_s.at[g], pair_hbm.at[g], out_sem.at[g])

    def out(g, _):
        for j in range(8):
            at = pl.multiple_of((g * 8 + j) * 64, 64)
            pair_s[g, j] = flat[pl.ds(at, 64), :].astype(BF)

        @pl.when(g > 0)
        def _():
            out_copy(g - 1).start()

        return 0

    lax.fori_loop(0, 16, out, 0)
    out_copy(15).start()
    for g in range(16):
        out_copy(g).wait()


def embed(z, coords, mask, wd, wb):
    any_spec = pl.BlockSpec(memory_space=pl.ANY)
    vmem = pl.BlockSpec(memory_space=pltpu.VMEM)
    dma = pltpu.SemaphoreType.DMA
    return pl.pallas_call(
        embed_kernel,
        out_shape=(
            jax.ShapeDtypeStruct((16, 8, 64, 128), BF),
            jax.ShapeDtypeStruct((4, 64, 128), F32),
        ),
        in_specs=[any_spec, vmem, vmem, vmem, vmem],
        out_specs=(any_spec, vmem),
        scratch_shapes=[
            pltpu.VMEM((64, 128, 128), BF),
            pltpu.VMEM((16, 8, 64, 128), BF),
            pltpu.VMEM((128, 128), BF),
            pltpu.VMEM((8, 128), F32),
            pltpu.VMEM((8, 128), F32),
            pltpu.VMEM((8, 128), F32),
            pltpu.VMEM((8, 8, 128), F32),
            pltpu.VMEM((16, 8, 128), F32),
            pltpu.VMEM((8192, 128), F32),
            dma((7,)), dma((7,)), dma((16,)), dma((16,)), dma, dma((16,)),
        ],
        compiler_params=pltpu.CompilerParams(collective_id=0, has_side_effects=True, vmem_limit_bytes=63 << 20),
        name="embed",
    )(z, coords, mask, wd, wb)


def place():
    row = lax.axis_index("row")
    col = lax.axis_index("col")
    core = lax.rem(row, 2)
    at = {"x": lax.rem(col, 4), "y": row // 4, "z": (col // 4) * 2 + lax.rem(row // 2, 2)}
    return row, col, core, at


def device_of(at, core):
    return (at["y"] * 4 + lax.rem(at["z"], 2) * 2 + core, (at["z"] // 2) * 4 + at["x"])


def beside(at, dim, delta):
    moved = dict(at)
    moved[dim] = lax.rem(at[dim] + delta + 4, 4)
    return moved


def of32(n):
    return pl.multiple_of(n, 32)


def main_kernel(pair_ref, bias_ref, wa_ref, wo_ref, d_ref, m_ref,
                xs, g0, g1, g2, q_s, k_s, v_s, g_s, s_s, m_s, acc_s, u_s, relay,
                asend, arecv, osem, send, recv, lsem, psend, precv,
                dsend, drecv, rsend, rrecv, msend, mrecv, hsem):
    row, col, core, at = place()
    gs = (g0, g1, g2)
    zh = col // 4
    yh = row // 8
    partner = device_of(at, 1 - core)
    looped = jnp.logical_and(yh == zh, core == yh)
    src_row0 = core * 8
    src_zh = yh
    slot = lax.rem(row, 8)
    barrier = pltpu.get_barrier_semaphore()

    def signal(device):
        pl.semaphore_signal(barrier, inc=1, device_id=device, device_id_type=MESH)

    def greet(d, _):
        signal((lax.rem(row + d, 16), col))
        return 0

    lax.fori_loop(1, 16, greet, 0)
    for dim in ("x", "y", "z"):
        for delta in (1, -1):
            signal(device_of(beside(at, dim, delta), core))
    signal(device_of(beside(at, "x", 2), core))
    signal(device_of(beside(at, "z", 2), core))

    def greet_relay(s, _):
        @pl.when(jnp.logical_or(src_row0 + s != row, src_zh != zh))
        def _():
            signal((src_row0 + s, src_zh * 4 + at["x"]))

        return 0

    lax.fori_loop(0, 8, greet_relay, 0)

    @pl.when(looped)
    def _():
        pl.semaphore_wait(barrier, 30)

    @pl.when(jnp.logical_not(looped))
    def _():
        pl.semaphore_wait(barrier, 31)

    def a2a(n, half):
        dy, dz, dc = SPREAD[n]
        to = lax.rem(at["y"] + dy, 4) * 4 + lax.rem(lax.rem(row // 2, 2) + dz, 2) * 2 + lax.rem(core + dc, 2)
        cols = pl.ds(half * 4, 4)
        return remote(
            pair_ref.at[to, cols], xs.at[row, cols], asend.at[half, n], arecv.at[half, n], (to, col)
        )

    def gather_copy(stage, p, k, t):
        dims = ORDERS[p]
        first, count = ROWS[p]
        g = gs[p]
        delta = (1, -1, 2)[k] if stage < 2 else (1, -1)[k % 2]
        a = [at[d] for d in dims]
        if stage == 2 and k >= 2:
            a[stage] = lax.rem(a[stage] - delta + 4, 4)
        a1, a2, a3 = a
        if stage == 0:
            src = bias_ref.at[t, pl.ds(first, count), :]
            dst = g.at[t, core, a3, a2, a1]
        else:
            src = g.at[t, core, a3, a2] if stage == 1 else g.at[t, core, a3]
            if stage == 2 and k >= 2:
                src = src.at[pl.ds(2 * (k % 2), 2)]
            dst = src
        n = p * 10 + stage * 3 + k
        return remote(src, dst, send.at[t, n], recv.at[t, n], device_of(beside(at, dims[stage], delta), core))

    def keep(p, t):
        a1, a2, a3 = (at[d] for d in ORDERS[p])
        first, count = ROWS[p]
        return pltpu.make_async_copy(
            bias_ref.at[t, pl.ds(first, count), :], gs[p].at[t, core, a3, a2, a1], lsem.at[t, p]
        )

    def share(p, k, t):
        a3 = lax.rem(at[ORDERS[p][2]] + (0, 3, 1, 2)[k], 4)
        plane = gs[p].at[t, core, a3]
        return remote(plane, plane, psend.at[t, p * 4 + k], precv.at[t, p * 4 + k], partner)

    def gather_step(n, t):
        parts = range(3)
        if n == 0:
            for p in parts:
                keep(p, t).start()
                for k in range(3):
                    gather_copy(0, p, k, t).start()
        elif n in (1, 2):
            for p in parts:
                if n == 1:
                    keep(p, t).wait()
                for k in range(3):
                    gather_copy(n - 1, p, k, t).wait_recv()
                for k in range(3 if n == 1 else 2):
                    gather_copy(n, p, k, t).start()
            if n == 2:
                for p in parts:
                    share(p, 0, t).start()
        elif n == 3:
            for p in parts:
                for k in (0, 1):
                    gather_copy(2, p, k, t).wait_recv()
                    gather_copy(2, p, k + 2, t).start()
            for p in parts:
                for k in (0, 1):
                    share(p, k + 1, t).start()
        elif n == 4:
            for p in parts:
                for k in (2, 3):
                    gather_copy(2, p, k, t).wait_recv()
                share(p, 3, t).start()
        else:
            for p in parts:
                for k in range(4):
                    share(p, k, t).wait()
                for stage in range(3):
                    for k in range(3 if stage < 2 else 4):
                        gather_copy(stage, p, k, t).wait_send()

    def direct(c, t):
        to = 2 * c + t // 2
        return (
            to,
            u_s.at[:, pl.ds(of32(c * 128 + t * 32), 32), :],
            d_ref.at[row, :, pl.ds(of32(lax.rem(t, 2) * 32), 32), :],
            dsend.at[t, c],
            drecv.at[lax.rem(t, 2), row],
        )

    def direct_remote(c, t):
        to, src, dst, s1, s2 = direct(c, t)
        return remote(src, dst, s1, s2, (to, col))

    def direct_local(c, t):
        to, src, dst, s1, s2 = direct(c, t)
        return pltpu.make_async_copy(src, dst, hsem.at[0, lax.rem(t, 2)])

    def direct_arrival(s, tt):
        return remote(
            u_s.at[:, pl.ds(0, 32), :], d_ref.at[s, :, pl.ds(of32(tt * 32), 32), :],
            dsend.at[0, 0], drecv.at[tt, s], (s, col),
        )

    def hop(delta, zz, t):
        x2 = lax.rem(at["x"] + delta, 4)
        c = zz * 4 + x2
        return remote(
            u_s.at[:, pl.ds(of32(c * 128 + t * 32), 32), :], relay.at[t, 3 - delta, zz],
            rsend.at[t, delta - 1, zz], rrecv.at[t, 3 - delta, zz], device_of(beside(at, "x", delta), core),
        )

    def hop_arrival(n, zz, t):
        return remote(
            u_s.at[:, pl.ds(0, 32), :], relay.at[t, n, zz],
            rsend.at[t, 2 - n, zz], rrecv.at[t, n, zz], device_of(beside(at, "x", n + 1), core),
        )

    def mirror(n, zz, t):
        sx = lax.rem(at["x"] + n, 4)
        to_row = 2 * (4 * zh + sx) + yh
        c = zz * 4 + at["x"]
        if n == 0:
            src = u_s.at[:, pl.ds(of32(c * 128 + t * 32), 32), :]
        else:
            src = relay.at[t, n - 1, zz]
        dst = m_ref.at[slot, :, pl.ds(of32(t * 32), 32), :]
        here = jnp.logical_and(to_row == row, zz == zh)
        rem = remote(src, dst, msend.at[t, n, zz], mrecv.at[t, slot], (to_row, c))
        loc = pltpu.make_async_copy(src, dst, hsem.at[1, t])
        return here, rem, loc

    def mirror_arrival(s, t):
        return remote(
            u_s.at[:, pl.ds(0, 32), :], m_ref.at[s, :, pl.ds(of32(t * 32), 32), :],
            msend.at[t, 0, 0], mrecv.at[t, s], (src_row0 + s, src_zh * 4 + at["x"]),
        )

    def either(here, if_here, otherwise):
        @pl.when(here)
        def _():
            if_here()

        @pl.when(jnp.logical_not(here))
        def _():
            otherwise()

    def exit_first(t, zz):
        for delta in (1, 2, 3):
            hop(delta, zz, t).start()
        here, rem, loc = mirror(0, zz, t)
        either(here, loc.start, rem.start)

        def go(n, _):
            c = zz * 4 + lax.rem(at["x"] + n, 4)
            either(
                2 * c + t // 2 == row, lambda: direct_local(c, t).start(), lambda: direct_remote(c, t).start()
            )
            return 0

        lax.fori_loop(0, 4, go, 0)

    def exit_second(t, zz):
        for n in (1, 2, 3):
            hop_arrival(n - 1, zz, t).wait_recv()
            here, rem, loc = mirror(n, zz, t)
            either(here, loc.start, rem.start)

    def project(j):
        p = jnp.dot(layer_norm(xs[:, j].reshape(1024, 128)), wa_ref[...], preferred_element_type=F32)
        q_s[j] = (p[:, :128] * (32**-0.5)).astype(BF)
        k_s[j] = p[:, 128:256].astype(BF)
        v_s[j] = p[:, 256:384].astype(BF).T
        g_s[j] = p[:, 384:].astype(BF)

    head_of_lane = lax.broadcasted_iota(jnp.int32, (32, 128), 1) // 32
    ones = jnp.ones((16, 256), BF)

    def bias_block(t, cp, kb, n):
        parts = []
        for zl in range(2):
            for cc in range(2):
                for p in range(3):
                    where = {"x": 2 * lax.rem(cp, 2) + n, "y": kb, "z": 2 * (cp // 2) + zl}
                    d1, d2, d3 = ORDERS[p]
                    parts.append(gs[p][t, cc, where[d3], where[d2], where[d1]])
        return jnp.concatenate(parts, axis=0)

    diagonal = lax.broadcasted_iota(jnp.int32, (128, 256), 0) // 32 == lax.rem(
        lax.broadcasted_iota(jnp.int32, (128, 256), 1) // 32, 4
    )
    fold_row = lax.broadcasted_iota(jnp.int32, (64, 256), 0)
    fold_lane = lax.broadcasted_iota(jnp.int32, (64, 256), 1)
    fold = jnp.where(
        jnp.logical_and(fold_row // 32 == fold_lane // 128, lax.rem(fold_row, 32) == lax.rem(fold_lane, 32)), 1.0, 0.0
    ).astype(BF)
    minor = (((1,), (1,)), ((), ()))

    def split(f):
        n = lax.rem(f, 32)
        first = f < 32
        cp = jnp.where(first, lax.rem(n, 16) // 4, n // 8)
        j = jnp.where(first, (n // 16) * 4 + lax.rem(n, 4), lax.rem(n, 8))
        return f // 32, cp, j

    def queries(t, cp, j):
        parts = []
        for n in range(2):
            q = q_s[j, pl.ds(of32((cp * 2 + n) * 128 + t * 32), 32), :]
            for h in range(4):
                parts.append(jnp.where(head_of_lane == h, q, jnp.zeros_like(q)))
        return jnp.concatenate(parts, axis=0)

    def score(t, cp, j, qm, kb):
        s = lax.dot_general(k_s[j, pl.ds(kb * 256, 256), :], qm, minor, preferred_element_type=F32)
        return s + jnp.concatenate([bias_block(t, cp, kb, 0), bias_block(t, cp, kb, 1)], axis=1)

    def score_block(b, t, cp, j, qm, kb, highest):
        s = score(t, cp, j, qm, kb)
        s_s[b, kb] = s
        here = jnp.max(s.reshape(32, 8, 256), axis=0)
        return here if highest is None else jnp.maximum(highest, here)

    def finish(t, cp, j, acc):
        att = jnp.where(diagonal, acc[:128] * (1.0 / acc[128:129]), 0.0)
        high = att.astype(BF)
        low = (att - high.astype(F32)).astype(BF)
        rows = lax.dot_general(fold, high, minor, preferred_element_type=F32)
        rows = rows + lax.dot_general(fold, low, minor, preferred_element_type=F32)
        firsts = [of32((cp * 2 + n) * 128 + t * 32) for n in range(2)]
        gate = jnp.concatenate([g_s[j, pl.ds(first, 32), :] for first in firsts], axis=0).astype(F32)
        gated = (rows / (1.0 + jnp.exp(-gate))).astype(BF)
        upd = jnp.dot(gated, wo_ref[...], preferred_element_type=F32)
        for n, first in enumerate(firsts):
            x = xs[(cp * 2 + n) * 2 + t // 2, j, pl.ds(of32(lax.rem(t, 2) * 32), 32), :]
            u_s[j, pl.ds(first, 32), :] = (x.astype(F32) + upd[n * 32 : n * 32 + 32]).astype(BF)

    def prologue():
        highest = None
        qm = queries(0, 0, 0)
        for kb in range(4):
            highest = score_block(0, 0, 0, 0, qm, kb, highest)
        m_s[0] = highest

    def task(f, b):
        t, cp, j = split(f)
        t2, cp2, j2 = split(jnp.minimum(f + 1, 127))
        t0, cp0, j0 = split(jnp.maximum(f - 1, 0))
        qm = queries(t2, cp2, j2)
        m = jnp.max(m_s[b], axis=0, keepdims=True)
        acc = None
        highest = None
        for kb in range(4):
            e = jnp.exp2((s_s[b, kb] - m) * LOG2E).astype(BF)
            highest = score_block(1 - b, t2, cp2, j2, qm, kb, highest)
            lhs = jnp.concatenate([v_s[j, :, kb * 256 : kb * 256 + 256], ones], axis=0)
            r = jnp.dot(lhs, e, preferred_element_type=F32)
            acc = r if acc is None else acc + r
            if kb == 1:
                finish(t0, cp0, j0, acc_s[1 - b])
        m_s[1 - b] = highest
        acc_s[b] = acc

    own = pltpu.make_async_copy(pair_ref.at[row], xs.at[row], osem)
    own.start()
    gather_step(0, 0)
    gather_step(0, 1)
    for n in range(1, 5):
        for d in range(8 * n - 8, min(8 * n, 30)):
            a2a(d % 15, d // 15).start()
        gather_step(n, 0)
        if n < 3:
            gather_step(n, 1)
    own.wait()
    for n in range(15):
        a2a(n, 0).wait()

    def prepare(j, _):
        for n, (chunk, step) in PREPARE.items():
            @pl.when(j == n)
            def _():
                gather_step(step, chunk)

        project(j)
        return 0

    lax.fori_loop(0, 4, prepare, 0)

    def chunk(t, _):
        def half(hh, _):
            for (tt, n), (later, step) in ATTEND.items():
                @pl.when(jnp.logical_and(hh == n, t == tt))
                def _():
                    gather_step(step, later)

            @pl.when(jnp.logical_and(hh == 3, t == 0))
            def _():
                for n in range(15):
                    a2a(n, 1).wait()

                def late(j, _):
                    project(j)
                    return 0

                lax.fori_loop(4, 8, late, 0)

            @pl.when(jnp.logical_and(hh == 0, t == 1))
            def _():
                exit_first(0, 0)

            @pl.when(jnp.logical_and(hh == 1, t > 0))
            def _():
                exit_first(t - 1, 1)

            @pl.when(jnp.logical_or(jnp.logical_and(hh == 0, t > 1), jnp.logical_and(hh == 3, t == 1)))
            def _():
                exit_second(t - 1, 0)

            @pl.when(jnp.logical_and(hh == 4, t > 0))
            def _():
                exit_second(t - 1, 1)

            @pl.when(jnp.logical_and(hh == 5, t > 0))
            def _():
                exit_first(t, 0)

            def two(i, _):
                task(t * 32 + hh * 4 + i * 2, 0)
                task(t * 32 + hh * 4 + i * 2 + 1, 1)
                return 0

            lax.fori_loop(0, 2, two, 0)
            return 0

        lax.fori_loop(0, 8, half, 0)
        return 0

    prologue()
    acc_s[1] = jnp.ones((144, 256), F32)
    lax.fori_loop(0, 4, chunk, 0)
    finish(3, 3, 7, acc_s[1])
    exit_first(3, 1)
    exit_second(3, 0)
    exit_second(3, 1)

    def drain(t, _):
        def one(c, _):
            either(
                2 * c + t // 2 == row, lambda: direct_local(c, t).wait(), lambda: direct_remote(c, t).wait_send()
            )
            return 0

        lax.fori_loop(0, 8, one, 0)
        for zz in range(2):
            for delta in (1, 2, 3):
                hop(delta, zz, t).wait_send()
            for n in range(4):
                here, rem, loc = mirror(n, zz, t)
                either(here, loc.wait, rem.wait_send)

        def arrived(s, _):
            @pl.when(jnp.logical_or(src_row0 + s != row, src_zh != zh))
            def _():
                mirror_arrival(s, t).wait_recv()

            return 0

        lax.fori_loop(0, 8, arrived, 0)
        return 0

    lax.fori_loop(0, 4, drain, 0)

    def landed(s, _):
        @pl.when(s != row)
        def _():
            for tt in range(2):
                direct_arrival(s, tt).wait_recv()

        return 0

    lax.fori_loop(0, 16, landed, 0)


def main(pair, bias, wa, wo):
    any_spec = pl.BlockSpec(memory_space=pl.ANY)
    vmem = pl.BlockSpec(memory_space=pltpu.VMEM)
    dma = pltpu.SemaphoreType.DMA
    return pl.pallas_call(
        main_kernel,
        out_shape=(jax.ShapeDtypeStruct((16, 8, 64, 128), BF), jax.ShapeDtypeStruct((8, 8, 128, 128), BF)),
        in_specs=[any_spec, vmem, vmem, vmem],
        out_specs=(any_spec,) * 2,
        scratch_shapes=[pltpu.VMEM((16, 8, 64, 128), BF)]
        + [pltpu.VMEM((4, 2, 4, 4, 4, n, 128), F32) for _, n in ROWS]
        + [
            pltpu.VMEM((8, 1024, 128), BF),
            pltpu.VMEM((8, 1024, 128), BF),
            pltpu.VMEM((8, 128, 1024), BF),
            pltpu.VMEM((8, 1024, 128), BF),
            pltpu.VMEM((2, 4, 256, 256), F32),
            pltpu.VMEM((2, 8, 256), F32),
            pltpu.VMEM((2, 144, 256), F32),
            pltpu.VMEM((8, 1024, 128), BF),
            pltpu.VMEM((4, 3, 2, 8, 32, 128), BF),
            dma((2, 15)), dma((2, 15)), dma,
            dma((4, 30)), dma((4, 30)), dma((4, 3)), dma((4, 12)), dma((4, 12)),
            dma((4, 8)), dma((2, 16)), dma((4, 3, 2)), dma((4, 3, 2)), dma((4, 4, 2)), dma((4, 8)), dma((2, 4)),
        ],
        compiler_params=pltpu.CompilerParams(collective_id=1, has_side_effects=True, vmem_limit_bytes=60 << 20),
        name="main",
    )(pair, bias, wa, wo)


def logits_kernel(d_ref, m_ref, wp_ref, we_ref, o_ref, flat, wp_s, we_s):
    @pl.when(pl.program_id(0) == 0)
    def _():
        wp_s[...] = jnp.zeros((128, 128), BF)
        we_s[...] = jnp.zeros((128, 128), BF)
        wp_s[0:64] = wp_ref[...]
        we_s[64:128] = we_ref[...]

    flat[...] = d_ref[...].reshape(1024, 128).astype(F32)
    u = jnp.concatenate([flat[pl.ds(a, 128, stride=8), :] for a in range(8)], axis=0)
    sym = u + m_ref[...].reshape(1024, 128).astype(F32)
    minor = (((1,), (1,)), ((), ()))
    pae = lax.dot_general(layer_norm(u), wp_s[...], minor, preferred_element_type=F32)
    pde = lax.dot_general(layer_norm(sym), we_s[...], minor, preferred_element_type=F32)
    o_ref[...] = (pae + pde).reshape(8, 128, 128)


def logits(d, m, wp, we):
    return pl.pallas_call(
        logits_kernel,
        grid=(8,),
        out_shape=jax.ShapeDtypeStruct((64, 128, 128), F32),
        in_specs=[
            pl.BlockSpec((16, 8, 8, 128), lambda t: (0, 0, t, 0)),
            pl.BlockSpec((8, 128, 128), lambda t: (t, 0, 0)),
            pl.BlockSpec((64, 128), lambda t: (0, 0)),
            pl.BlockSpec((64, 128), lambda t: (0, 0)),
        ],
        out_specs=pl.BlockSpec((8, 128, 128), lambda t: (t, 0, 0)),
        scratch_shapes=[pltpu.VMEM((1024, 128), F32), pltpu.VMEM((128, 128), BF), pltpu.VMEM((128, 128), BF)],
        compiler_params=pltpu.CompilerParams(vmem_limit_bytes=63 << 20),
        name="logits",
    )(d, m, wp, we)


def per_device(z_trunk, coords, token_mask, w_dist, w_attn, w_bias, w_out, w_pae, w_pde):
    pair, bias = embed(z_trunk, coords, token_mask[None], w_dist, w_bias.T)
    direct, mirror = main(pair, bias, w_attn, w_out)
    return logits(direct, mirror.reshape(64, 128, 128), w_pae.T, w_pde.T)


def solution(mesh):
    in_specs = (P("row", "col", None), P(None, ("row", "col")), P(("row", "col")), P(), P(), P(), P(), P(), P())
    return jax.shard_map(
        per_device, mesh=mesh, in_specs=in_specs, out_specs=P("row", "col", None), check_vma=False
    )
```

```python
import functools

import jax
import jax.numpy as jnp
from jax import lax
from jax.experimental import pallas as pl
from jax.experimental.pallas import tpu as pltpu
from jax.sharding import PartitionSpec as P

MESH = pl.DeviceIdType.MESH
BF = jnp.bfloat16
F32 = jnp.float32
LOG2E = 1.4426950408889634
ORDERS = (("y", "z", "x"), ("z", "x", "y"), ("x", "y", "z"))
ROWS = ((0, 24), (24, 24), (48, 16))
SPREAD = (
    (1, 0, 0), (3, 0, 0), (0, 1, 0), (2, 0, 0), (1, 1, 0), (3, 1, 0), (0, 0, 1), (2, 1, 0),
    (1, 0, 1), (3, 0, 1), (0, 1, 1), (2, 0, 1), (1, 1, 1), (3, 1, 1), (2, 1, 1),
)
PREPARE = {0: (1, 3), 1: (2, 0), 3: (0, 5)}
ATTEND = {
    (0, 0): (1, 4), (0, 1): (2, 1), (0, 2): (2, 2), (0, 3): (3, 0), (0, 4): (1, 5), (0, 5): (2, 3), (0, 6): (3, 1),
    (1, 0): (2, 4), (1, 1): (3, 2), (1, 3): (2, 5), (1, 4): (3, 3), (1, 7): (3, 4), (2, 2): (3, 5),
}


def layer_norm(values):
    widened = values.astype(F32)
    average = jnp.mean(widened, axis=-1, keepdims=True)
    centred = widened - average
    variance = jnp.mean(centred * centred, axis=-1, keepdims=True)
    return (centred * lax.rsqrt(variance + 1e-05)).astype(BF)


def remote(src, dst, send, recv, device):
    return pltpu.make_async_remote_copy(
        src_ref=src, dst_ref=dst, send_sem=send, recv_sem=recv, device_id=device, device_id_type=MESH
    )


def embed_kernel(z_hbm, coords_ref, mask_ref, wd_raw, wb_ref, pair_hbm, bias_ref,
                 z_ref, pair_s, wd_ref, info, sub_ref, lane_ref, rs, rl, flat,
                 s_send, s_recv, l_send, l_recv, z_sem, out_sem):
    load_z = pltpu.make_async_copy(z_hbm, z_ref, z_sem)
    load_z.start()
    row = lax.axis_index("row")
    col = lax.axis_index("col")
    slot = lax.rem(row, 2) * 8 + col
    target = row // 2
    info[...] = jnp.zeros((8, 128), F32)
    info[0:3, 0:8] = coords_ref[...].astype(F32)
    info[3:4, 0:8] = mask_ref[...].astype(F32)
    tokens = info[...]
    sub_ref[...] = jnp.concatenate([tokens] * 16, axis=0).T[0:8]
    lane_ref[...] = pltpu.roll(tokens, slot * 8, 1)
    wd_ref[...] = jnp.zeros((128, 128), BF)
    wd_ref[0:39] = wd_raw[...]
    barrier = pltpu.get_barrier_semaphore()

    def greet_row(d, _):
        pl.semaphore_signal(barrier, inc=1, device_id=(row, lax.rem(col + d, 8)), device_id_type=MESH)
        return 0

    lax.fori_loop(1, 8, greet_row, 0)

    def greet_source(s, _):
        src_row = 2 * col + s // 8
        src_col = lax.rem(s, 8)

        @pl.when(jnp.logical_or(src_row != row, src_col != col))
        def _():
            pl.semaphore_signal(barrier, inc=1, device_id=(src_row, src_col), device_id_type=MESH)

        return 0

    lax.fori_loop(0, 16, greet_source, 0)

    @pl.when(target == col)
    def _():
        pl.semaphore_wait(barrier, 22)

    @pl.when(target != col)
    def _():
        pl.semaphore_wait(barrier, 23)

    def row_copy(d):
        to = lax.rem(col + d, 8)
        return remote(sub_ref, rs.at[col], s_send.at[d - 1], s_recv.at[d - 1], (row, to))

    def lane_copy(r):
        return remote(lane_ref, rl.at[slot], l_send.at[r], l_recv.at[slot], (r, target))

    def lane_arrival(s):
        return remote(lane_ref, rl.at[s], l_send.at[s], l_recv.at[s], (2 * col + s // 8, lax.rem(s, 8)))

    def start_row(d, _):
        row_copy(d).start()
        return 0

    lax.fori_loop(1, 8, start_row, 0)

    def start_lane(r, _):
        @pl.when(jnp.logical_or(r != row, target != col))
        def _():
            lane_copy(r).start()

        return 0

    lax.fori_loop(0, 16, start_lane, 0)
    rs[col] = sub_ref[...]

    @pl.when(target == col)
    def _():
        rl[slot] = lane_ref[...]

    def wait_row(d, _):
        row_copy(d).wait()
        return 0

    lax.fori_loop(1, 8, wait_row, 0)

    def wait_lane(r, _):
        @pl.when(jnp.logical_or(r != row, target != col))
        def _():
            lane_copy(r).wait_send()

        @pl.when(jnp.logical_or(2 * col + r // 8 != row, lax.rem(r, 8) != col))
        def _():
            lane_arrival(r).wait_recv()

        return 0

    lax.fori_loop(0, 16, wait_lane, 0)

    lanes = jnp.sum(rl[...], axis=0)
    turned = jnp.concatenate([lanes] * 16, axis=0).T
    cx, cy, cz = (jnp.broadcast_to(turned[:, n : n + 1], (128, 128)) for n in range(3))
    edge = lax.broadcasted_iota(jnp.int32, (1, 128), 1)
    upper_edge = 27 + 4 * edge
    lower_edge = 23 + 4 * edge
    big = jnp.int32(1 << 20)
    lower = jnp.where(edge == 0, -1, jnp.where(edge >= 39, big, lower_edge * lower_edge)).astype(F32)
    upper = jnp.where(edge >= 38, big, upper_edge * upper_edge).astype(F32)
    head = lax.broadcasted_iota(jnp.int32, (8, 128), 1) // 32

    load_z.wait()

    def eight(t, _):
        own = rs[t]
        key_bias = (own[:, 3:4] - 1.0) * 30000.0
        hots = []
        for a in range(8):
            dx = cx - own[a : a + 1, 0:1]
            dy = cy - own[a : a + 1, 1:2]
            dz = cz - own[a : a + 1, 2:3]
            squared = dx * dx + dy * dy + dz * dz
            hots.append(jnp.where(jnp.logical_and(squared > lower, squared <= upper), 1.0, 0.0).astype(BF))
        added = jnp.dot(jnp.concatenate(hots, axis=0), wd_ref[...], preferred_element_type=F32)
        start = pl.multiple_of(t * 8, 8)
        z = z_ref[pl.ds(start, 8)].reshape(1024, 128).astype(F32)
        pair = (z + added).astype(BF)
        wide = pair.astype(F32)
        for a in range(8):
            flat[pl.ds(start + a, 128, stride=64), :] = wide[a * 128 : a * 128 + 128]
        normed = layer_norm(pair)
        b = lax.dot_general(wb_ref[...], normed, (((1,), (1,)), ((), ())), preferred_element_type=F32)
        by_head = [
            jnp.concatenate([b[h : h + 1, a * 128 : a * 128 + 128] for a in range(8)], axis=0) + key_bias
            for h in range(4)
        ]
        for c in range(4):
            moved = [pltpu.roll(by_head[h], (32 * h - 32 * c) % 128, 1) for h in range(4)]
            block = moved[3]
            for h in (2, 1, 0):
                block = jnp.where(head == h, moved[h], block)
            bias_ref[c, pl.ds(start, 8), :] = block
        return 0

    lax.fori_loop(0, 8, eight, 0, unroll=4)

    def out_copy(g):
        return pltpu.make_async_copy(pair_s.at[g], pair_hbm.at[g], out_sem.at[g])

    def out(g, _):
        for j in range(8):
            at = pl.multiple_of((g * 8 + j) * 64, 64)
            pair_s[g, j] = flat[pl.ds(at, 64), :].astype(BF)

        @pl.when(g > 0)
        def _():
            out_copy(g - 1).start()

        return 0

    lax.fori_loop(0, 16, out, 0)
    out_copy(15).start()
    for g in range(16):
        out_copy(g).wait()


def embed(z, coords, mask, wd, wb):
    any_spec = pl.BlockSpec(memory_space=pl.ANY)
    vmem = pl.BlockSpec(memory_space=pltpu.VMEM)
    dma = pltpu.SemaphoreType.DMA
    return pl.pallas_call(
        embed_kernel,
        out_shape=(
            jax.ShapeDtypeStruct((16, 8, 64, 128), BF),
            jax.ShapeDtypeStruct((4, 64, 128), F32),
        ),
        in_specs=[any_spec, vmem, vmem, vmem, vmem],
        out_specs=(any_spec, vmem),
        scratch_shapes=[
            pltpu.VMEM((64, 128, 128), BF),
            pltpu.VMEM((16, 8, 64, 128), BF),
            pltpu.VMEM((128, 128), BF),
            pltpu.VMEM((8, 128), F32),
            pltpu.VMEM((8, 128), F32),
            pltpu.VMEM((8, 128), F32),
            pltpu.VMEM((8, 8, 128), F32),
            pltpu.VMEM((16, 8, 128), F32),
            pltpu.VMEM((8192, 128), F32),
            dma((7,)), dma((7,)), dma((16,)), dma((16,)), dma, dma((16,)),
        ],
        compiler_params=pltpu.CompilerParams(collective_id=0, has_side_effects=True, vmem_limit_bytes=63 << 20),
        name="embed",
    )(z, coords, mask, wd, wb)


def place():
    row = lax.axis_index("row")
    col = lax.axis_index("col")
    core = lax.rem(row, 2)
    at = {"x": lax.rem(col, 4), "y": row // 4, "z": (col // 4) * 2 + lax.rem(row // 2, 2)}
    return row, col, core, at


def device_of(at, core):
    return (at["y"] * 4 + lax.rem(at["z"], 2) * 2 + core, (at["z"] // 2) * 4 + at["x"])


def beside(at, dim, delta):
    moved = dict(at)
    moved[dim] = lax.rem(at[dim] + delta + 4, 4)
    return moved


def of32(n):
    return pl.multiple_of(n, 32)


def main_kernel(pair_ref, bias_ref, wa_ref, wo_ref, d_ref, m_ref,
                xs, g0, g1, g2, q_s, k_s, v_s, g_s, s_s, m_s, acc_s, u_s, relay,
                asend, arecv, osem, send, recv, lsem, psend, precv,
                dsend, drecv, rsend, rrecv, msend, mrecv, hsem):
    row, col, core, at = place()
    gs = (g0, g1, g2)
    zh = col // 4
    yh = row // 8
    partner = device_of(at, 1 - core)
    looped = jnp.logical_and(yh == zh, core == yh)
    src_row0 = core * 8
    src_zh = yh
    slot = lax.rem(row, 8)
    barrier = pltpu.get_barrier_semaphore()

    def signal(device):
        pl.semaphore_signal(barrier, inc=1, device_id=device, device_id_type=MESH)

    def greet(d, _):
        signal((lax.rem(row + d, 16), col))
        return 0

    lax.fori_loop(1, 16, greet, 0)
    for dim in ("x", "y", "z"):
        for delta in (1, -1):
            signal(device_of(beside(at, dim, delta), core))
    signal(device_of(beside(at, "x", 2), core))
    signal(device_of(beside(at, "z", 2), core))

    def greet_relay(s, _):
        @pl.when(jnp.logical_or(src_row0 + s != row, src_zh != zh))
        def _():
            signal((src_row0 + s, src_zh * 4 + at["x"]))

        return 0

    lax.fori_loop(0, 8, greet_relay, 0)

    @pl.when(looped)
    def _():
        pl.semaphore_wait(barrier, 30)

    @pl.when(jnp.logical_not(looped))
    def _():
        pl.semaphore_wait(barrier, 31)

    def a2a(n, half):
        dy, dz, dc = SPREAD[n]
        to = lax.rem(at["y"] + dy, 4) * 4 + lax.rem(lax.rem(row // 2, 2) + dz, 2) * 2 + lax.rem(core + dc, 2)
        cols = pl.ds(half * 4, 4)
        return remote(
            pair_ref.at[to, cols], xs.at[row, cols], asend.at[half, n], arecv.at[half, n], (to, col)
        )

    def gather_copy(stage, p, k, t):
        dims = ORDERS[p]
        first, count = ROWS[p]
        g = gs[p]
        delta = (1, -1, 2)[k] if stage < 2 else (1, -1)[k % 2]
        a = [at[d] for d in dims]
        if stage == 2 and k >= 2:
            a[stage] = lax.rem(a[stage] - delta + 4, 4)
        a1, a2, a3 = a
        if stage == 0:
            src = bias_ref.at[t, pl.ds(first, count), :]
            dst = g.at[t, core, a3, a2, a1]
        else:
            src = g.at[t, core, a3, a2] if stage == 1 else g.at[t, core, a3]
            if stage == 2 and k >= 2:
                src = src.at[pl.ds(2 * (k % 2), 2)]
            dst = src
        n = p * 10 + stage * 3 + k
        return remote(src, dst, send.at[t, n], recv.at[t, n], device_of(beside(at, dims[stage], delta), core))

    def keep(p, t):
        a1, a2, a3 = (at[d] for d in ORDERS[p])
        first, count = ROWS[p]
        return pltpu.make_async_copy(
            bias_ref.at[t, pl.ds(first, count), :], gs[p].at[t, core, a3, a2, a1], lsem.at[t, p]
        )

    def share(p, k, t):
        a3 = lax.rem(at[ORDERS[p][2]] + (0, 3, 1, 2)[k], 4)
        plane = gs[p].at[t, core, a3]
        return remote(plane, plane, psend.at[t, p * 4 + k], precv.at[t, p * 4 + k], partner)

    def gather_step(n, t):
        parts = range(3)
        if n == 0:
            for p in parts:
                keep(p, t).start()
                for k in range(3):
                    gather_copy(0, p, k, t).start()
        elif n in (1, 2):
            for p in parts:
                if n == 1:
                    keep(p, t).wait()
                for k in range(3):
                    gather_copy(n - 1, p, k, t).wait_recv()
                for k in range(3 if n == 1 else 2):
                    gather_copy(n, p, k, t).start()
            if n == 2:
                for p in parts:
                    share(p, 0, t).start()
        elif n == 3:
            for p in parts:
                for k in (0, 1):
                    gather_copy(2, p, k, t).wait_recv()
                    gather_copy(2, p, k + 2, t).start()
            for p in parts:
                for k in (0, 1):
                    share(p, k + 1, t).start()
        elif n == 4:
            for p in parts:
                for k in (2, 3):
                    gather_copy(2, p, k, t).wait_recv()
                share(p, 3, t).start()
        else:
            for p in parts:
                for k in range(4):
                    share(p, k, t).wait()
                for stage in range(3):
                    for k in range(3 if stage < 2 else 4):
                        gather_copy(stage, p, k, t).wait_send()

    def direct(c, t):
        to = 2 * c + t // 2
        return (
            to,
            u_s.at[:, pl.ds(of32(c * 128 + t * 32), 32), :],
            d_ref.at[row, :, pl.ds(of32(lax.rem(t, 2) * 32), 32), :],
            dsend.at[t, c],
            drecv.at[lax.rem(t, 2), row],
        )

    def direct_remote(c, t):
        to, src, dst, s1, s2 = direct(c, t)
        return remote(src, dst, s1, s2, (to, col))

    def direct_local(c, t):
        to, src, dst, s1, s2 = direct(c, t)
        return pltpu.make_async_copy(src, dst, hsem.at[0, lax.rem(t, 2)])

    def direct_arrival(s, tt):
        return remote(
            u_s.at[:, pl.ds(0, 32), :], d_ref.at[s, :, pl.ds(of32(tt * 32), 32), :],
            dsend.at[0, 0], drecv.at[tt, s], (s, col),
        )

    def hop(delta, zz, t):
        x2 = lax.rem(at["x"] + delta, 4)
        c = zz * 4 + x2
        return remote(
            u_s.at[:, pl.ds(of32(c * 128 + t * 32), 32), :], relay.at[t, 3 - delta, zz],
            rsend.at[t, delta - 1, zz], rrecv.at[t, 3 - delta, zz], device_of(beside(at, "x", delta), core),
        )

    def hop_arrival(n, zz, t):
        return remote(
            u_s.at[:, pl.ds(0, 32), :], relay.at[t, n, zz],
            rsend.at[t, 2 - n, zz], rrecv.at[t, n, zz], device_of(beside(at, "x", n + 1), core),
        )

    def mirror(n, zz, t):
        sx = lax.rem(at["x"] + n, 4)
        to_row = 2 * (4 * zh + sx) + yh
        c = zz * 4 + at["x"]
        if n == 0:
            src = u_s.at[:, pl.ds(of32(c * 128 + t * 32), 32), :]
        else:
            src = relay.at[t, n - 1, zz]
        dst = m_ref.at[slot, :, pl.ds(of32(t * 32), 32), :]
        here = jnp.logical_and(to_row == row, zz == zh)
        rem = remote(src, dst, msend.at[t, n, zz], mrecv.at[t, slot], (to_row, c))
        loc = pltpu.make_async_copy(src, dst, hsem.at[1, t])
        return here, rem, loc

    def mirror_arrival(s, t):
        return remote(
            u_s.at[:, pl.ds(0, 32), :], m_ref.at[s, :, pl.ds(of32(t * 32), 32), :],
            msend.at[t, 0, 0], mrecv.at[t, s], (src_row0 + s, src_zh * 4 + at["x"]),
        )

    def either(here, if_here, otherwise):
        @pl.when(here)
        def _():
            if_here()

        @pl.when(jnp.logical_not(here))
        def _():
            otherwise()

    def exit_first(t, zz):
        for delta in (1, 2, 3):
            hop(delta, zz, t).start()
        here, rem, loc = mirror(0, zz, t)
        either(here, loc.start, rem.start)

        def go(n, _):
            c = zz * 4 + lax.rem(at["x"] + n, 4)
            either(
                2 * c + t // 2 == row, lambda: direct_local(c, t).start(), lambda: direct_remote(c, t).start()
            )
            return 0

        lax.fori_loop(0, 4, go, 0)

    def exit_second(t, zz):
        for n in (1, 2, 3):
            hop_arrival(n - 1, zz, t).wait_recv()
            here, rem, loc = mirror(n, zz, t)
            either(here, loc.start, rem.start)

    def project(j):
        p = jnp.dot(layer_norm(xs[:, j].reshape(1024, 128)), wa_ref[...], preferred_element_type=F32)
        q_s[j] = (p[:, :128] * (32**-0.5)).astype(BF)
        k_s[j] = p[:, 128:256].astype(BF)
        v_s[j] = p[:, 256:384].astype(BF).T
        g_s[j] = p[:, 384:].astype(BF)

    head_of_lane = lax.broadcasted_iota(jnp.int32, (32, 128), 1) // 32
    ones = jnp.ones((16, 256), BF)

    def bias_block(t, cp, kb, n):
        parts = []
        for zl in range(2):
            for cc in range(2):
                for p in range(3):
                    where = {"x": 2 * lax.rem(cp, 2) + n, "y": kb, "z": 2 * (cp // 2) + zl}
                    d1, d2, d3 = ORDERS[p]
                    parts.append(gs[p][t, cc, where[d3], where[d2], where[d1]])
        return jnp.concatenate(parts, axis=0)

    diagonal = lax.broadcasted_iota(jnp.int32, (128, 256), 0) // 32 == lax.rem(
        lax.broadcasted_iota(jnp.int32, (128, 256), 1) // 32, 4
    )
    fold_row = lax.broadcasted_iota(jnp.int32, (64, 256), 0)
    fold_lane = lax.broadcasted_iota(jnp.int32, (64, 256), 1)
    fold = jnp.where(
        jnp.logical_and(fold_row // 32 == fold_lane // 128, lax.rem(fold_row, 32) == lax.rem(fold_lane, 32)), 1.0, 0.0
    ).astype(BF)
    minor = (((1,), (1,)), ((), ()))

    def split(f):
        n = lax.rem(f, 32)
        first = f < 32
        cp = jnp.where(first, lax.rem(n, 16) // 4, n // 8)
        j = jnp.where(first, (n // 16) * 4 + lax.rem(n, 4), lax.rem(n, 8))
        return f // 32, cp, j

    def queries(t, cp, j):
        parts = []
        for n in range(2):
            q = q_s[j, pl.ds(of32((cp * 2 + n) * 128 + t * 32), 32), :]
            for h in range(4):
                parts.append(jnp.where(head_of_lane == h, q, jnp.zeros_like(q)))
        return jnp.concatenate(parts, axis=0)

    def score(t, cp, j, qm, kb):
        s = lax.dot_general(k_s[j, pl.ds(kb * 256, 256), :], qm, minor, preferred_element_type=F32)
        return s + jnp.concatenate([bias_block(t, cp, kb, 0), bias_block(t, cp, kb, 1)], axis=1)

    def score_block(b, t, cp, j, qm, kb, highest):
        s = score(t, cp, j, qm, kb)
        s_s[b, kb] = s
        here = jnp.max(s.reshape(32, 8, 256), axis=0)
        return here if highest is None else jnp.maximum(highest, here)

    def finish(t, cp, j, acc):
        att = jnp.where(diagonal, acc[:128] * (1.0 / acc[128:129]), 0.0)
        high = att.astype(BF)
        low = (att - high.astype(F32)).astype(BF)
        rows = lax.dot_general(fold, high, minor, preferred_element_type=F32)
        rows = rows + lax.dot_general(fold, low, minor, preferred_element_type=F32)
        firsts = [of32((cp * 2 + n) * 128 + t * 32) for n in range(2)]
        gate = jnp.concatenate([g_s[j, pl.ds(first, 32), :] for first in firsts], axis=0).astype(F32)
        gated = (rows / (1.0 + jnp.exp(-gate))).astype(BF)
        upd = jnp.dot(gated, wo_ref[...], preferred_element_type=F32)
        for n, first in enumerate(firsts):
            x = xs[(cp * 2 + n) * 2 + t // 2, j, pl.ds(of32(lax.rem(t, 2) * 32), 32), :]
            u_s[j, pl.ds(first, 32), :] = (x.astype(F32) + upd[n * 32 : n * 32 + 32]).astype(BF)

    def prologue():
        highest = None
        qm = queries(0, 0, 0)
        for kb in range(4):
            highest = score_block(0, 0, 0, 0, qm, kb, highest)
        m_s[0] = highest

    def task(f, b):
        t, cp, j = split(f)
        t2, cp2, j2 = split(jnp.minimum(f + 1, 127))
        t0, cp0, j0 = split(jnp.maximum(f - 1, 0))
        qm = queries(t2, cp2, j2)
        m = jnp.max(m_s[b], axis=0, keepdims=True)
        acc = None
        highest = None
        for kb in range(4):
            e = jnp.exp2((s_s[b, kb] - m) * LOG2E).astype(BF)
            highest = score_block(1 - b, t2, cp2, j2, qm, kb, highest)
            lhs = jnp.concatenate([v_s[j, :, kb * 256 : kb * 256 + 256], ones], axis=0)
            r = jnp.dot(lhs, e, preferred_element_type=F32)
            acc = r if acc is None else acc + r
            if kb == 1:
                finish(t0, cp0, j0, acc_s[1 - b])
        m_s[1 - b] = highest
        acc_s[b] = acc

    own = pltpu.make_async_copy(pair_ref.at[row], xs.at[row], osem)
    own.start()
    gather_step(0, 0)
    gather_step(0, 1)
    for n in range(1, 5):
        for d in range(8 * n - 8, min(8 * n, 30)):
            a2a(d % 15, d // 15).start()
        gather_step(n, 0)
        if n < 3:
            gather_step(n, 1)
    own.wait()
    for n in range(15):
        a2a(n, 0).wait()

    def prepare(j, _):
        for n, (chunk, step) in PREPARE.items():
            @pl.when(j == n)
            def _():
                gather_step(step, chunk)

        project(j)
        return 0

    lax.fori_loop(0, 4, prepare, 0, unroll=2)

    def chunk(t, _):
        def half(hh, _):
            for (tt, n), (later, step) in ATTEND.items():
                @pl.when(jnp.logical_and(hh == n, t == tt))
                def _():
                    gather_step(step, later)

            @pl.when(jnp.logical_and(hh == 3, t == 0))
            def _():
                for n in range(15):
                    a2a(n, 1).wait()

                def late(j, _):
                    project(j)
                    return 0

                lax.fori_loop(4, 8, late, 0, unroll=2)

            @pl.when(jnp.logical_and(hh == 0, t == 1))
            def _():
                exit_first(0, 0)

            @pl.when(jnp.logical_and(hh == 1, t > 0))
            def _():
                exit_first(t - 1, 1)

            @pl.when(jnp.logical_or(jnp.logical_and(hh == 2, t > 1), jnp.logical_and(hh == 3, t == 1)))
            def _():
                exit_second(t - 1, 0)

            @pl.when(jnp.logical_and(hh == 5, t > 0))
            def _():
                exit_second(t - 1, 1)

            @pl.when(jnp.logical_and(hh == 5, t > 0))
            def _():
                exit_first(t, 0)

            def two(i, _):
                task(t * 32 + hh * 4 + i * 2, 0)
                task(t * 32 + hh * 4 + i * 2 + 1, 1)
                return 0

            lax.fori_loop(0, 2, two, 0)
            return 0

        lax.fori_loop(0, 8, half, 0)
        return 0

    prologue()
    acc_s[1] = jnp.ones((144, 256), F32)
    lax.fori_loop(0, 4, chunk, 0)
    finish(3, 3, 7, acc_s[1])
    exit_first(3, 1)
    exit_second(3, 0)
    exit_second(3, 1)

    def drain(t, _):
        def one(c, _):
            either(
                2 * c + t // 2 == row, lambda: direct_local(c, t).wait(), lambda: direct_remote(c, t).wait_send()
            )
            return 0

        lax.fori_loop(0, 8, one, 0)
        for zz in range(2):
            for delta in (1, 2, 3):
                hop(delta, zz, t).wait_send()
            for n in range(4):
                here, rem, loc = mirror(n, zz, t)
                either(here, loc.wait, rem.wait_send)

        def arrived(s, _):
            @pl.when(jnp.logical_or(src_row0 + s != row, src_zh != zh))
            def _():
                mirror_arrival(s, t).wait_recv()

            return 0

        lax.fori_loop(0, 8, arrived, 0)
        return 0

    lax.fori_loop(0, 4, drain, 0)

    def landed(s, _):
        @pl.when(s != row)
        def _():
            for tt in range(2):
                direct_arrival(s, tt).wait_recv()

        return 0

    lax.fori_loop(0, 16, landed, 0)


def main(pair, bias, wa, wo):
    any_spec = pl.BlockSpec(memory_space=pl.ANY)
    vmem = pl.BlockSpec(memory_space=pltpu.VMEM)
    dma = pltpu.SemaphoreType.DMA
    return pl.pallas_call(
        main_kernel,
        out_shape=(jax.ShapeDtypeStruct((16, 8, 64, 128), BF), jax.ShapeDtypeStruct((8, 8, 128, 128), BF)),
        in_specs=[any_spec, vmem, vmem, vmem],
        out_specs=(any_spec,) * 2,
        scratch_shapes=[pltpu.VMEM((16, 8, 64, 128), BF)]
        + [pltpu.VMEM((4, 2, 4, 4, 4, n, 128), F32) for _, n in ROWS]
        + [
            pltpu.VMEM((8, 1024, 128), BF),
            pltpu.VMEM((8, 1024, 128), BF),
            pltpu.VMEM((8, 128, 1024), BF),
            pltpu.VMEM((8, 1024, 128), BF),
            pltpu.VMEM((2, 4, 256, 256), F32),
            pltpu.VMEM((2, 8, 256), F32),
            pltpu.VMEM((2, 144, 256), F32),
            pltpu.VMEM((8, 1024, 128), BF),
            pltpu.VMEM((4, 3, 2, 8, 32, 128), BF),
            dma((2, 15)), dma((2, 15)), dma,
            dma((4, 30)), dma((4, 30)), dma((4, 3)), dma((4, 12)), dma((4, 12)),
            dma((4, 8)), dma((2, 16)), dma((4, 3, 2)), dma((4, 3, 2)), dma((4, 4, 2)), dma((4, 8)), dma((2, 4)),
        ],
        compiler_params=pltpu.CompilerParams(collective_id=1, has_side_effects=True, vmem_limit_bytes=60 << 20),
        name="main",
    )(pair, bias, wa, wo)


def logits_kernel(d_ref, m_ref, wp_ref, we_ref, o_ref, flat, wp_s, we_s):
    @pl.when(pl.program_id(0) == 0)
    def _():
        wp_s[...] = jnp.zeros((128, 128), BF)
        we_s[...] = jnp.zeros((128, 128), BF)
        wp_s[0:64] = wp_ref[...]
        we_s[64:128] = we_ref[...]

    flat[...] = d_ref[...].reshape(1024, 128).astype(F32)
    u = jnp.concatenate([flat[pl.ds(a, 128, stride=8), :] for a in range(8)], axis=0)
    sym = u + m_ref[...].reshape(1024, 128).astype(F32)
    minor = (((1,), (1,)), ((), ()))
    pae = lax.dot_general(layer_norm(u), wp_s[...], minor, preferred_element_type=F32)
    pde = lax.dot_general(layer_norm(sym), we_s[...], minor, preferred_element_type=F32)
    o_ref[...] = (pae + pde).reshape(8, 128, 128)


def logits(d, m, wp, we):
    return pl.pallas_call(
        logits_kernel,
        grid=(8,),
        out_shape=jax.ShapeDtypeStruct((64, 128, 128), F32),
        in_specs=[
            pl.BlockSpec((16, 8, 8, 128), lambda t: (0, 0, t, 0)),
            pl.BlockSpec((8, 128, 128), lambda t: (t, 0, 0)),
            pl.BlockSpec((64, 128), lambda t: (0, 0)),
            pl.BlockSpec((64, 128), lambda t: (0, 0)),
        ],
        out_specs=pl.BlockSpec((8, 128, 128), lambda t: (t, 0, 0)),
        scratch_shapes=[pltpu.VMEM((1024, 128), F32), pltpu.VMEM((128, 128), BF), pltpu.VMEM((128, 128), BF)],
        compiler_params=pltpu.CompilerParams(vmem_limit_bytes=63 << 20),
        name="logits",
    )(d, m, wp, we)


def per_device(z_trunk, coords, token_mask, w_dist, w_attn, w_bias, w_out, w_pae, w_pde):
    pair, bias = embed(z_trunk, coords, token_mask[None], w_dist, w_bias.T)
    direct, mirror = main(pair, bias, w_attn, w_out)
    return logits(direct, mirror.reshape(64, 128, 128), w_pae.T, w_pde.T)


def solution(mesh):
    in_specs = (P("row", "col", None), P(None, ("row", "col")), P(("row", "col")), P(), P(), P(), P(), P(), P())
    return jax.shard_map(
        per_device, mesh=mesh, in_specs=in_specs, out_specs=P("row", "col", None), check_vma=False
    )
```
